32 devices in a mesh: aux: 4 (over y, x), blk: 4 (over z), occ: 2 (over core).
Axes of the slice: x: 2, y: 2, z: 4, core: 2. Of those that a mesh axis runs over, the one named last changes fastest.
Arguments:
- integrals: bfloat16 [16, 4, 11, 512, 512], P('aux', 'blk'), may hold values from -0.078125 to 0.078125
- orbitals: bfloat16 [2048, 512], P('blk', 'occ'), may hold values from -6 to 6
- pair_lists: int32 [4, 11], P('blk'), may hold values from 0 to 3, as said below
- pair_counts: int32 [4], P('blk'), may hold values from 1 to 11, as said below
Outputs:
- exchange: float32 [4, 512, 512], P('blk', 'aux')
The draws below stay inside these ranges and needn't reach their ends.
Inputs may be any that keep to these rules, and one draw needn't show every extreme that they name: `pair_lists`: entry 0 of row m is m itself; entries past pair_counts[m] are never read. `pair_counts`: some block has all 11 slots live.
All inputs are finite; a program needn't handle non-finite values.
Results may differ from the reference program's by a relative error of at most 0.00099.
Values may be sent and summed in bfloat16 or wider, within the bound.
No kernel may reach another device: no remote copies, remote signals or barrier semaphores. Data moves between devices by JAX's collectives and lax.ppermute only.
A program may use at most 192 MiB of HBM per device.

```python
import jax
import jax.numpy as jnp
from jax import lax

BS = 512
SLOTS = 11
NOCC = 512
NB = 4
NBAS = 2048
NAUX = 16


def fullest_block(key):
    return jax.random.randint(jax.random.fold_in(key, 29), (), 0, NB)


def draw_pair_lists(key, part):
    values = jax.random.randint(jax.random.fold_in(key, 11), (NB, SLOTS), 0, NB)
    rows = jnp.arange(NB, dtype=jnp.int32)
    far_block = (rows + NB // 2) % NB
    choose_far = jax.random.randint(jax.random.fold_in(key, 37), (NB,), 0, 2) == 1
    choose_far = choose_far | (rows == fullest_block(key))
    values = values.at[:, 1].set(jnp.where(choose_far, far_block, values[:, 1]))
    return values.at[:, 0].set(rows).astype(jnp.int32)


def draw_pair_counts(key, part):
    counts = jax.random.randint(jax.random.fold_in(key, 23), (NB,), 1, SLOTS + 1)
    return counts.at[fullest_block(key)].set(SLOTS).astype(jnp.int32)


def steps_of(own_key, extent, split, low, high):
    factor_of = 1.0
    for position, blocks in split:
        steps = jax.random.uniform(jax.random.fold_in(jax.random.fold_in(own_key, 6), position), (blocks,), jnp.float32, low / len(split), high / len(split))
        factor_of = factor_of * jnp.repeat(jnp.exp(steps), extent[position] // blocks).reshape((-1,) + (1,) * (len(extent) - 1 - position))
    return factor_of


def normal_values(key, shape, spread, bound, split=(), held_as=jnp.bfloat16):
    result = jax.random.normal(key, shape, jnp.float32) * spread
    if len(split) > 0:
        result = steps_of(key, shape, split, -0.22, 0.18) * result
    return jnp.clip(result, min=-bound, max=bound).astype(held_as)


def setup_inputs(seed: int = 0) -> dict:
    splits = jax.random.split(jax.random.key(seed), 5)
    return {
        "integrals": normal_values(splits[0], (NAUX, NB, SLOTS, BS, BS), (BS * SLOTS) ** -0.5, 0.078125, ((0, 4), (1, 4))),
        "orbitals": normal_values(splits[1], (NBAS, NOCC), 1.0, 6.0, ((0, 4), (1, 2))),
        "pair_lists": draw_pair_lists(jax.random.fold_in(splits[4], 71), 0),
        "pair_counts": draw_pair_counts(jax.random.fold_in(splits[4], 71), 0),
    }


def reference(integrals, orbitals, pair_lists, pair_counts):
    coef_blocks = orbitals.reshape(NB, BS, NOCC)

    def one_block(block_index):
        block_ints = lax.dynamic_index_in_dim(integrals, block_index, 1, keepdims=False)
        lists = lax.dynamic_index_in_dim(pair_lists, block_index, 0, keepdims=False)
        live = lax.dynamic_index_in_dim(pair_counts, block_index, 0, keepdims=False)
        picked = coef_blocks[lists.astype(jnp.int32)]
        keep = (jnp.arange(SLOTS, dtype=jnp.int32) < live).astype(jnp.float32)
        picked = picked.astype(jnp.float32) * keep[:, None, None]
        half = jnp.einsum("psab,sbi->pai", block_ints.astype(jnp.float32), picked)
        half = half.astype(jnp.bfloat16).astype(jnp.float32)
        return jnp.einsum("pai,pbi->ab", half, half) / NOCC

    return lax.map(one_block, jnp.arange(NB, dtype=jnp.int32))
```

```python
import functools
import math

import jax
import jax.numpy as jnp
from jax import lax
from jax.experimental import pallas as pl
from jax.experimental.pallas import tpu as pltpu
from jax.sharding import PartitionSpec as P


ANY = pl.BlockSpec(memory_space=pl.ANY)
VMEM = pl.BlockSpec(memory_space=pltpu.VMEM)
SMEM = pl.BlockSpec(memory_space=pltpu.SMEM)


def exchange_pairs(distance, size):
    return [(i, i ^ distance) for i in range(size)]


def accumulate_slots(lo, hi, lists_ref, counts_ref, ints_ref, coef_ref, acc_ref, buffer, sems, order, started):
    aux_total, _, slot_total, width, _ = ints_ref.shape
    me = lax.axis_index("blk")
    live = counts_ref[0]
    found = jnp.int32(0)
    for slot in range(slot_total):
        away = lists_ref[0, slot] ^ me
        order[found] = slot
        found = found + ((slot < live) & (away >= lo) & (away < hi)).astype(jnp.int32)

    def fetch(i):
        return pltpu.make_async_copy(ints_ref.at[:, 0, order[i]], buffer.at[i], sems.at[i])

    @pl.loop(0, found)
    def _(i):
        fetch(i).start()

    started()

    @pl.loop(0, found)
    def _(i):
        fetch(i).wait()
        away = lists_ref[0, order[i]] ^ me
        rows = pl.ds(pl.multiple_of((away - lo) * width, width), width)

        @pl.loop(0, aux_total)
        def _(p):
            acc_ref[p] += jnp.dot(buffer[i, p], coef_ref[rows, :], preferred_element_type=jnp.float32)


def near_kernel(lo, first, lists_ref, counts_ref, ints_ref, coef_ref, *rest):
    if first:
        acc_ref, buffer, sems, order = rest

        def started():
            acc_ref[...] = jnp.zeros_like(acc_ref)

    else:
        old_ref, acc_ref, buffer, sems, order = rest

        def started():
            acc_ref[...] = old_ref[...]

    accumulate_slots(
        lo, lo + 1, lists_ref, counts_ref, ints_ref, coef_ref, acc_ref, buffer, sems, order, started
    )


def far_kernel(lo, hi, lists_ref, counts_ref, ints_ref, old_ref, *rest):
    aux_size, occ_size = lax.axis_size("aux"), lax.axis_size("occ")
    chunks = rest[:aux_size]
    pieces = rest[aux_size : aux_size + occ_size]
    coef, acc_ref, halves, buffer, sems, chunk_sems, order = rest[aux_size + occ_size :]
    my_aux, my_occ = lax.axis_index("aux"), lax.axis_index("occ")
    depth = chunks[0].shape[0]

    def started():
        copies = []
        for k in range(aux_size):
            rows = pl.ds(pl.multiple_of((my_aux ^ k) * depth, depth), depth)
            copies.append(pltpu.make_async_copy(chunks[k], coef.at[rows], chunk_sems.at[k]))
        for copy in copies:
            copy.start()
        acc_ref[...] = old_ref[...]
        for copy in copies:
            copy.wait()

    accumulate_slots(
        lo, hi, lists_ref, counts_ref, ints_ref, coef, acc_ref, buffer, sems, order, started
    )
    columns = acc_ref.shape[2]
    for p in range(acc_ref.shape[0]):
        halves[:, p * columns : (p + 1) * columns] = acc_ref[p].astype(jnp.bfloat16)
    share = pieces[0].shape[1]
    for k in range(occ_size):
        rows = pl.ds(pl.multiple_of((my_occ ^ k) * share, share), share)
        pieces[k][...] = lax.dot_general(
            halves[...], halves[rows, :], (((1,), (1,)), ((), ())), preferred_element_type=jnp.float32
        )


def split_kernel(*refs):
    aux_size, occ_size = lax.axis_size("aux"), lax.axis_size("occ")
    terms, outs = refs[:occ_size], refs[occ_size:]
    my_aux = lax.axis_index("aux")
    depth = outs[0].shape[0]
    for k in range(aux_size):
        rows = pl.ds(pl.multiple_of((my_aux ^ k) * depth, depth), depth)
        total = terms[0][rows, :]
        for term in terms[1:]:
            total = total + term[rows, :]
        outs[k][...] = total


def per_device(integrals, orbitals, pair_lists, pair_counts):
    aux_total, _, slot_total, width, _ = integrals.shape
    columns = orbitals.shape[1]
    aux_size, blk_size, occ_size = (lax.axis_size(n) for n in ("aux", "blk", "occ"))
    my_aux, my_occ = lax.axis_index("aux"), lax.axis_index("occ")
    slot_flops = 2 * aux_total * width * width * columns
    slot_bytes = 2 * aux_total * width * width
    limit = 44 << 20

    depth = (blk_size - 2) * width // aux_size
    piece = math.gcd(depth, width)
    parts = []
    for t in range(depth // piece):
        starts = [a * depth + t * piece for a in range(aux_size)]
        pairs = [
            (a * blk_size + i, a * blk_size + (i ^ (2 + starts[a] // width)))
            for a in range(aux_size)
            for i in range(blk_size)
        ]
        offset = (my_aux * depth + t * piece) % width
        sent = lax.dynamic_slice_in_dim(orbitals, offset, piece, 0)
        parts.append(lax.ppermute(sent, ("aux", "blk"), pairs))
    next_block = lax.ppermute(orbitals, "blk", exchange_pairs(1, blk_size))
    chunk = parts[0] if len(parts) == 1 else jnp.concatenate(parts, 0)
    chunks = [chunk] + [
        lax.ppermute(chunk, "aux", exchange_pairs(k, aux_size)) for k in range(1, aux_size)
    ]

    acc_shape = jax.ShapeDtypeStruct((aux_total, width, columns), jnp.float32)
    slot_scratch = [
        pltpu.VMEM((slot_total, aux_total, width, width), jnp.bfloat16),
        pltpu.SemaphoreType.DMA((slot_total,)),
    ]
    order = pltpu.SMEM((slot_total + 1,), jnp.int32)

    def near(lo, coef, *old):
        return pl.pallas_call(
            functools.partial(near_kernel, lo, not old),
            out_shape=acc_shape,
            in_specs=[SMEM, SMEM, ANY, VMEM] + [VMEM] * len(old),
            out_specs=VMEM,
            scratch_shapes=slot_scratch + [order],
            compiler_params=pltpu.CompilerParams(vmem_limit_bytes=limit),
            cost_estimate=pl.CostEstimate(
                flops=3 * slot_flops, bytes_accessed=3 * slot_bytes, transcendentals=0
            ),
            name=f"near_{lo}",
        )(pair_lists, pair_counts, integrals, coef, *old)

    acc = near(0, orbitals)
    acc = near(1, next_block, acc)

    share = width // occ_size
    pieces = pl.pallas_call(
        functools.partial(far_kernel, 2, blk_size),
        out_shape=[jax.ShapeDtypeStruct((width, share), jnp.float32)] * occ_size,
        in_specs=[SMEM, SMEM, ANY, VMEM] + [ANY] * aux_size,
        out_specs=[VMEM] * occ_size,
        scratch_shapes=[
            pltpu.VMEM(((blk_size - 2) * width, columns), jnp.bfloat16),
            pltpu.VMEM((aux_total, width, columns), jnp.float32),
            pltpu.VMEM((width, aux_total * columns), jnp.bfloat16),
        ]
        + slot_scratch
        + [pltpu.SemaphoreType.DMA((aux_size,)), order],
        compiler_params=pltpu.CompilerParams(vmem_limit_bytes=limit),
        cost_estimate=pl.CostEstimate(
            flops=6 * slot_flops, bytes_accessed=6 * slot_bytes, transcendentals=0
        ),
        name="far",
    )(pair_lists, pair_counts, integrals, acc, *chunks)

    terms = [pieces[0]] + [
        lax.ppermute(pieces[k], "occ", exchange_pairs(k, occ_size)) for k in range(1, occ_size)
    ]
    rows = width // aux_size
    mine = pl.pallas_call(
        split_kernel,
        out_shape=[jax.ShapeDtypeStruct((rows, share), jnp.float32)] * aux_size,
        in_specs=[VMEM] * occ_size,
        out_specs=[VMEM] * aux_size,
        compiler_params=pltpu.CompilerParams(vmem_limit_bytes=8 << 20),
        name="split",
    )(*terms)
    total = mine[0]
    for k in range(1, aux_size):
        total = total + lax.ppermute(mine[k], "aux", exchange_pairs(k, aux_size))
    total = total / (columns * occ_size)
    shares = [total] + [
        lax.ppermute(total, "occ", exchange_pairs(k, occ_size)) for k in range(1, occ_size)
    ]
    ordered = []
    for o in range(occ_size):
        value = shares[0]
        for k in range(1, occ_size):
            value = jnp.where((my_occ ^ k) == o, shares[k], value)
        ordered.append(value)
    return jnp.concatenate(ordered, 1)[None]


def solution(mesh):
    placed = (P("aux", "blk", None, None, None), P("blk", "occ"), P("blk", None), P("blk"))
    return jax.shard_map(
        per_device, mesh=mesh, in_specs=placed, out_specs=P("blk", "aux", None), check_vma=False
    )
```

```python
import functools
import math

import jax
import jax.numpy as jnp
from jax import lax
from jax.experimental import pallas as pl
from jax.experimental.pallas import tpu as pltpu
from jax.sharding import PartitionSpec as P


ANY = pl.BlockSpec(memory_space=pl.ANY)
VMEM = pl.BlockSpec(memory_space=pltpu.VMEM)
SMEM = pl.BlockSpec(memory_space=pltpu.SMEM)
HBM = pl.BlockSpec(memory_space=pltpu.HBM)


def exchange_pairs(distance, size):
    return [(i, i ^ distance) for i in range(size)]


def in_hbm(x):
    return pltpu.with_memory_space_constraint(x, pltpu.HBM)


def slot_product(block_ref, coef):
    aux_total, width, _ = block_ref.shape
    flat = block_ref[...].reshape(aux_total * width, width)
    product = jnp.dot(flat, coef, preferred_element_type=jnp.float32)
    return product.reshape(aux_total, width, coef.shape[1])


def own_kernel(early, counts, lists_hbm, ints_ref, coef_hbm, acc_ref, buffer, table, coef, lists, sems, slot_sems):
    slot_total = ints_ref.shape[2]
    lists_copy = pltpu.make_async_copy(lists_hbm, lists, sems.at[0])
    lists_copy.start()
    coef_copy = pltpu.make_async_copy(coef_hbm, coef, sems.at[1])

    def fetch(i, slot):
        return pltpu.make_async_copy(ints_ref.at[:, 0, slot], buffer.at[i], slot_sems.at[i])

    fetch(0, 0).start()
    coef_copy.start()
    lists_copy.wait()
    me = lax.axis_index("blk")
    live = counts[0]
    found = jnp.int32(0)
    for step, (lo, hi) in enumerate(((0, 1), (1, 2), (2, 1 << 30))):
        for slot in range(slot_total):
            away = lists[0, slot] ^ me
            table[found] = slot
            table[slot_total + 1 + found] = away
            found = found + ((slot < live) & (away >= lo) & (away < hi)).astype(jnp.int32)
        table[2 * slot_total + 2 + step] = found
    own = jnp.minimum(table[2 * slot_total + 2], early)
    ready = jnp.minimum(live, early)

    @pl.loop(1, ready)
    def _(i):
        fetch(i, table[i]).start()

    coef_copy.wait()
    fetch(0, 0).wait()
    acc_ref[...] = slot_product(buffer.at[0], coef[...])

    @pl.loop(1, own)
    def _(i):
        fetch(i, table[i]).wait()
        acc_ref[...] += slot_product(buffer.at[i], coef[...])

    @pl.loop(own, ready)
    def _(i):
        fetch(i, table[i]).wait()


def next_kernel(early, table, ints_ref, own_hbm, next_ref, _acc, _buffer, acc_ref, buffer, coef, sems, slot_sems):
    slot_total, _, width, _ = buffer.shape
    own, near, live = (table[2 * slot_total + 2 + step] for step in range(3))

    def fetch(i):
        return pltpu.make_async_copy(ints_ref.at[:, 0, table[i]], buffer.at[i], slot_sems.at[i])

    coef_copies = [
        pltpu.make_async_copy(own_hbm, coef.at[pl.ds(0, width)], sems.at[0]),
        pltpu.make_async_copy(next_ref, coef.at[pl.ds(width, width)], sems.at[1]),
    ]
    for copy in coef_copies:
        copy.start()

    @pl.loop(early, jnp.maximum(live, early))
    def _(i):
        fetch(i).start()

    for copy in coef_copies:
        copy.wait()

    @pl.loop(jnp.minimum(own, early), near)
    def _(i):
        @pl.when(i >= early)
        def _():
            fetch(i).wait()

        rows = pl.ds(pl.multiple_of(table[slot_total + 1 + i] * width, width), width)
        acc_ref[...] += slot_product(buffer.at[i], coef[rows, :])

    @pl.loop(jnp.maximum(near, early), jnp.maximum(live, early))
    def _(i):
        fetch(i).wait()


def far_kernel(table, buffer, _acc, *rest):
    aux_size, occ_size = lax.axis_size("aux"), lax.axis_size("occ")
    chunks = rest[:aux_size]
    pieces = rest[aux_size : aux_size + occ_size]
    total, coef, halves, sems = rest[aux_size + occ_size :]
    slot_total, _, width, _ = buffer.shape
    near, live = table[2 * slot_total + 3], table[2 * slot_total + 4]
    my_aux, my_occ = lax.axis_index("aux"), lax.axis_index("occ")
    depth = chunks[0].shape[0]
    copies = []
    for k in range(aux_size):
        rows = pl.ds(pl.multiple_of((my_aux ^ k) * depth, depth), depth)
        copies.append(pltpu.make_async_copy(chunks[k], coef.at[rows], sems.at[k]))
    for copy in copies:
        copy.start()
    for copy in copies:
        copy.wait()

    @pl.loop(near, live)
    def _(i):
        rows = pl.ds(pl.multiple_of((table[slot_total + 1 + i] - 2) * width, width), width)
        total[...] += slot_product(buffer.at[i], coef[rows, :])

    columns = total.shape[2]
    for p in range(total.shape[0]):
        halves[:, p * columns : (p + 1) * columns] = total[p].astype(jnp.bfloat16)
    share = pieces[0].shape[1]
    for k in range(occ_size):
        rows = pl.ds(pl.multiple_of((my_occ ^ k) * share, share), share)
        pieces[k][...] = lax.dot_general(
            halves[...], halves[rows, :], (((1,), (1,)), ((), ())), preferred_element_type=jnp.float32
        )


def split_kernel(*refs):
    aux_size, occ_size = lax.axis_size("aux"), lax.axis_size("occ")
    terms, outs = refs[:occ_size], refs[occ_size:]
    my_aux = lax.axis_index("aux")
    depth = outs[0].shape[0]
    for k in range(aux_size):
        rows = pl.ds(pl.multiple_of((my_aux ^ k) * depth, depth), depth)
        total = terms[0][rows, :]
        for term in terms[1:]:
            total = total + term[rows, :]
        outs[k][...] = total


def per_device(integrals, orbitals, pair_lists, pair_counts):
    aux_total, _, slot_total, width, _ = integrals.shape
    columns = orbitals.shape[1]
    aux_size, blk_size, occ_size = (lax.axis_size(n) for n in ("aux", "blk", "occ"))
    my_aux, my_occ = lax.axis_index("aux"), lax.axis_index("occ")
    slot_flops = 2 * aux_total * width * width * columns
    slot_bytes = 2 * aux_total * width * width
    early = (slot_total + 1) // 2

    def cost(slots):
        return pl.CostEstimate(
            flops=slots * slot_flops, bytes_accessed=slots * slot_bytes, transcendentals=0
        )

    depth = (blk_size - 2) * width // aux_size
    piece = math.gcd(depth, width)
    parts = []
    for t in range(depth // piece):
        starts = [a * depth + t * piece for a in range(aux_size)]
        pairs = [
            (a * blk_size + i, a * blk_size + (i ^ (2 + starts[a] // width)))
            for a in range(aux_size)
            for i in range(blk_size)
        ]
        offset = (my_aux * depth + t * piece) % width
        sent = lax.dynamic_slice_in_dim(orbitals, offset, piece, 0)
        parts.append(lax.ppermute(sent, ("aux", "blk"), pairs))
    next_block = lax.ppermute(orbitals, "blk", exchange_pairs(1, blk_size))
    chunk = parts[0] if len(parts) == 1 else jnp.concatenate(parts, 0)
    chunks = [chunk] + [
        lax.ppermute(chunk, "aux", exchange_pairs(k, aux_size)) for k in range(1, aux_size)
    ]

    acc_shape = jax.ShapeDtypeStruct((aux_total, width, columns), jnp.float32)
    buffer_shape = jax.ShapeDtypeStruct((slot_total, aux_total, width, width), jnp.bfloat16)
    table_shape = jax.ShapeDtypeStruct((2 * slot_total + 5,), jnp.int32)
    slot_sems = pltpu.SemaphoreType.DMA((slot_total,))

    acc, buffer, table = pl.pallas_call(
        functools.partial(own_kernel, early),
        out_shape=(acc_shape, buffer_shape, table_shape),
        in_specs=[SMEM, HBM, HBM, HBM],
        out_specs=(VMEM, VMEM, SMEM),
        scratch_shapes=[
            pltpu.VMEM((width, columns), jnp.bfloat16),
            pltpu.SMEM(pair_lists.shape, jnp.int32),
            pltpu.SemaphoreType.DMA((2,)),
            slot_sems,
        ],
        compiler_params=pltpu.CompilerParams(vmem_limit_bytes=8 << 20),
        cost_estimate=cost(early),
        name="own",
    )(pair_counts, in_hbm(pair_lists), in_hbm(integrals), in_hbm(orbitals))
    acc, buffer = pl.pallas_call(
        functools.partial(next_kernel, early),
        out_shape=(acc_shape, buffer_shape),
        in_specs=[SMEM, HBM, HBM, ANY, VMEM, VMEM],
        out_specs=(VMEM, VMEM),
        scratch_shapes=[
            pltpu.VMEM((2 * width, columns), jnp.bfloat16),
            pltpu.SemaphoreType.DMA((2,)),
            slot_sems,
        ],
        input_output_aliases={4: 0, 5: 1},
        compiler_params=pltpu.CompilerParams(vmem_limit_bytes=8 << 20),
        cost_estimate=cost(early),
        name="next",
    )(table, in_hbm(integrals), in_hbm(orbitals), next_block, acc, buffer)

    share = width // occ_size
    *pieces, _ = pl.pallas_call(
        far_kernel,
        out_shape=[jax.ShapeDtypeStruct((width, share), jnp.float32)] * occ_size + [acc_shape],
        in_specs=[SMEM, VMEM, VMEM] + [ANY] * aux_size,
        out_specs=[VMEM] * (occ_size + 1),
        scratch_shapes=[
            pltpu.VMEM(((blk_size - 2) * width, columns), jnp.bfloat16),
            pltpu.VMEM((width, aux_total * columns), jnp.bfloat16),
            pltpu.SemaphoreType.DMA((aux_size,)),
        ],
        input_output_aliases={2: occ_size},
        compiler_params=pltpu.CompilerParams(
            vmem_limit_bytes=(6 << 20) + 2 * columns * width * (blk_size - 2)
        ),
        cost_estimate=cost(early),
        name="far",
    )(table, buffer, acc, *chunks)

    terms = [pieces[0]] + [
        lax.ppermute(pieces[k], "occ", exchange_pairs(k, occ_size)) for k in range(1, occ_size)
    ]
    rows = width // aux_size
    mine = pl.pallas_call(
        split_kernel,
        out_shape=[jax.ShapeDtypeStruct((rows, share), jnp.float32)] * aux_size,
        in_specs=[VMEM] * occ_size,
        out_specs=[VMEM] * aux_size,
        compiler_params=pltpu.CompilerParams(vmem_limit_bytes=8 << 20),
        name="split",
    )(*terms)
    total = mine[0]
    for k in range(1, aux_size):
        total = total + lax.ppermute(mine[k], "aux", exchange_pairs(k, aux_size))
    total = total / (columns * occ_size)
    shares = [total] + [
        lax.ppermute(total, "occ", exchange_pairs(k, occ_size)) for k in range(1, occ_size)
    ]
    ordered = []
    for o in range(occ_size):
        value = shares[0]
        for k in range(1, occ_size):
            value = jnp.where((my_occ ^ k) == o, shares[k], value)
        ordered.append(value)
    return jnp.concatenate(ordered, 1)[None]


def solution(mesh):
    placed = (P("aux", "blk", None, None, None), P("blk", "occ"), P("blk", None), P("blk"))
    return jax.shard_map(
        per_device, mesh=mesh, in_specs=placed, out_specs=P("blk", "aux", None), check_vma=False
    )
```

```python
import functools
import math

import jax
import jax.numpy as jnp
from jax import lax
from jax.experimental import pallas as pl
from jax.experimental.pallas import tpu as pltpu
from jax.sharding import PartitionSpec as P


ANY = pl.BlockSpec(memory_space=pl.ANY)
VMEM = pl.BlockSpec(memory_space=pltpu.VMEM)
SMEM = pl.BlockSpec(memory_space=pltpu.SMEM)
HBM = pl.BlockSpec(memory_space=pltpu.HBM)


def exchange_pairs(distance, size):
    return [(i, i ^ distance) for i in range(size)]


def in_hbm(x):
    return pltpu.with_memory_space_constraint(x, pltpu.HBM)


def slot_product(block_ref, coef):
    aux_total, width, _ = block_ref.shape
    flat = block_ref[...].reshape(aux_total * width, width)
    product = jnp.dot(flat, coef, preferred_element_type=jnp.float32)
    return product.reshape(aux_total, width, coef.shape[1])


def add_far(table, i, distance, buffer, chunk_ref, acc_ref):
    slot_total, aux_total, width, _ = buffer.shape
    depth, columns = chunk_ref.shape
    piece = math.gcd(depth, width)
    base = (lax.axis_index("aux") ^ distance) * depth
    for part in range(width // piece):
        local = (table[slot_total + 1 + i] - 2) * width + part * piece - base

        @pl.when((local >= 0) & (local < depth))
        def _():
            left = buffer[i, :, :, part * piece : (part + 1) * piece]
            right = chunk_ref[pl.ds(pl.multiple_of(local, piece), piece), :]
            product = jnp.dot(
                left.reshape(aux_total * width, piece), right, preferred_element_type=jnp.float32
            )
            acc_ref[...] += product.reshape(aux_total, width, columns)


def own_kernel(early, counts, lists_hbm, ints_ref, coef_hbm, acc_ref, buffer, table, coef, lists, sems, slot_sems):
    slot_total = ints_ref.shape[2]
    lists_copy = pltpu.make_async_copy(lists_hbm, lists, sems.at[0])
    lists_copy.start()
    coef_copy = pltpu.make_async_copy(coef_hbm, coef, sems.at[1])

    def fetch(i, slot):
        return pltpu.make_async_copy(ints_ref.at[:, 0, slot], buffer.at[i], slot_sems.at[i])

    fetch(0, 0).start()
    coef_copy.start()
    lists_copy.wait()
    me = lax.axis_index("blk")
    live = counts[0]
    found = jnp.int32(0)
    for step, (lo, hi) in enumerate(((0, 1), (1, 2), (2, 1 << 30))):
        for slot in range(slot_total):
            away = lists[0, slot] ^ me
            table[found] = slot
            table[slot_total + 1 + found] = away
            found = found + ((slot < live) & (away >= lo) & (away < hi)).astype(jnp.int32)
        table[2 * slot_total + 2 + step] = found
    own = jnp.minimum(table[2 * slot_total + 2], early)
    ready = jnp.minimum(live, early)

    @pl.loop(1, ready)
    def _(i):
        fetch(i, table[i]).start()

    coef_copy.wait()
    fetch(0, 0).wait()
    acc_ref[...] = slot_product(buffer.at[0], coef[...])

    @pl.loop(1, own)
    def _(i):
        fetch(i, table[i]).wait()
        acc_ref[...] += slot_product(buffer.at[i], coef[...])

    @pl.loop(own, ready)
    def _(i):
        fetch(i, table[i]).wait()


def next_kernel(early, table, ints_ref, own_hbm, next_ref, chunk_ref, _acc, _buffer, acc_ref, buffer, coef, sems, slot_sems):
    slot_total, _, width, _ = buffer.shape
    own, near, live = (table[2 * slot_total + 2 + step] for step in range(3))

    def fetch(i):
        return pltpu.make_async_copy(ints_ref.at[:, 0, table[i]], buffer.at[i], slot_sems.at[i])

    coef_copies = [
        pltpu.make_async_copy(own_hbm, coef.at[pl.ds(0, width)], sems.at[0]),
        pltpu.make_async_copy(next_ref, coef.at[pl.ds(width, width)], sems.at[1]),
    ]
    for copy in coef_copies:
        copy.start()

    @pl.loop(early, jnp.maximum(live, early))
    def _(i):
        fetch(i).start()

    for copy in coef_copies:
        copy.wait()

    @pl.loop(jnp.minimum(own, early), near)
    def _(i):
        @pl.when(i >= early)
        def _():
            fetch(i).wait()

        rows = pl.ds(pl.multiple_of(table[slot_total + 1 + i] * width, width), width)
        acc_ref[...] += slot_product(buffer.at[i], coef[rows, :])

    @pl.loop(near, live)
    def _(i):
        @pl.when(i >= early)
        def _():
            fetch(i).wait()

        add_far(table, i, 0, buffer, chunk_ref, acc_ref)


def far_kernel(distance, table, buffer, chunk_ref, _acc, acc_ref):
    slot_total = buffer.shape[0]

    @pl.loop(table[2 * slot_total + 3], table[2 * slot_total + 4])
    def _(i):
        add_far(table, i, distance, buffer, chunk_ref, acc_ref)


def last_kernel(distance, table, buffer, chunk_ref, _acc, acc_ref, halves, *pieces):
    far_kernel(distance, table, buffer, chunk_ref, _acc, acc_ref)
    columns = acc_ref.shape[2]
    for p in range(acc_ref.shape[0]):
        halves[:, p * columns : (p + 1) * columns] = acc_ref[p].astype(jnp.bfloat16)
    for k, piece_ref in enumerate(pieces, 1):
        share_kernel(k, halves, piece_ref)


def share_kernel(distance, halves, piece_ref):
    share = piece_ref.shape[1]
    start = (lax.axis_index("occ") ^ distance) * share
    rows = pl.ds(pl.multiple_of(start, share), share)
    piece_ref[...] = lax.dot_general(
        halves[...], halves[rows, :], (((1,), (1,)), ((), ())), preferred_element_type=jnp.float32
    )


def split_kernel(*refs):
    aux_size, occ_size = lax.axis_size("aux"), lax.axis_size("occ")
    terms, outs = refs[:occ_size], refs[occ_size:]
    my_aux = lax.axis_index("aux")
    depth = outs[0].shape[0]
    for k in range(aux_size):
        rows = pl.ds(pl.multiple_of((my_aux ^ k) * depth, depth), depth)
        total = terms[0][rows, :]
        for term in terms[1:]:
            total = total + term[rows, :]
        outs[k][...] = total


def per_device(integrals, orbitals, pair_lists, pair_counts):
    aux_total, _, slot_total, width, _ = integrals.shape
    columns = orbitals.shape[1]
    aux_size, blk_size, occ_size = (lax.axis_size(n) for n in ("aux", "blk", "occ"))
    my_aux, my_occ = lax.axis_index("aux"), lax.axis_index("occ")
    slot_flops = 2 * aux_total * width * width * columns
    slot_bytes = 2 * aux_total * width * width
    early = (slot_total + 2) // 4

    def cost(slots):
        return pl.CostEstimate(
            flops=slots * slot_flops, bytes_accessed=slots * slot_bytes, transcendentals=0
        )

    depth = (blk_size - 2) * width // aux_size
    piece = math.gcd(depth, width)
    parts = []
    for t in range(depth // piece):
        starts = [a * depth + t * piece for a in range(aux_size)]
        pairs = [
            (a * blk_size + i, a * blk_size + (i ^ (2 + starts[a] // width)))
            for a in range(aux_size)
            for i in range(blk_size)
        ]
        offset = (my_aux * depth + t * piece) % width
        sent = lax.dynamic_slice_in_dim(orbitals, offset, piece, 0)
        parts.append(lax.ppermute(sent, ("aux", "blk"), pairs))
    next_block = lax.ppermute(orbitals, "blk", exchange_pairs(1, blk_size))
    chunk = parts[0] if len(parts) == 1 else jnp.concatenate(parts, 0)
    chunks = [chunk] + [
        lax.ppermute(chunk, "aux", exchange_pairs(k, aux_size)) for k in range(1, aux_size)
    ]

    acc_shape = jax.ShapeDtypeStruct((aux_total, width, columns), jnp.float32)
    buffer_shape = jax.ShapeDtypeStruct((slot_total, aux_total, width, width), jnp.bfloat16)
    table_shape = jax.ShapeDtypeStruct((2 * slot_total + 5,), jnp.int32)
    slot_sems = pltpu.SemaphoreType.DMA((slot_total,))

    acc, buffer, table = pl.pallas_call(
        functools.partial(own_kernel, early),
        out_shape=(acc_shape, buffer_shape, table_shape),
        in_specs=[SMEM, HBM, HBM, HBM],
        out_specs=(VMEM, VMEM, SMEM),
        scratch_shapes=[
            pltpu.VMEM((width, columns), jnp.bfloat16),
            pltpu.SMEM(pair_lists.shape, jnp.int32),
            pltpu.SemaphoreType.DMA((2,)),
            slot_sems,
        ],
        compiler_params=pltpu.CompilerParams(vmem_limit_bytes=8 << 20),
        cost_estimate=cost(early),
        name="own",
    )(pair_counts, in_hbm(pair_lists), in_hbm(integrals), in_hbm(orbitals))
    acc, buffer = pl.pallas_call(
        functools.partial(next_kernel, early),
        out_shape=(acc_shape, buffer_shape),
        in_specs=[SMEM, HBM, HBM, ANY, VMEM, VMEM, VMEM],
        out_specs=(VMEM, VMEM),
        scratch_shapes=[
            pltpu.VMEM((2 * width, columns), jnp.bfloat16),
            pltpu.SemaphoreType.DMA((2,)),
            slot_sems,
        ],
        input_output_aliases={5: 0, 6: 1},
        compiler_params=pltpu.CompilerParams(vmem_limit_bytes=8 << 20),
        cost_estimate=cost(early),
        name="next",
    )(table, in_hbm(integrals), in_hbm(orbitals), next_block, chunk, acc, buffer)

    share = width // occ_size
    piece_shape = jax.ShapeDtypeStruct((width, share), jnp.float32)
    halves_shape = jax.ShapeDtypeStruct((width, aux_total * columns), jnp.bfloat16)
    small = pltpu.CompilerParams(vmem_limit_bytes=8 << 20)
    for k in range(1, aux_size - 1):
        acc = pl.pallas_call(
            functools.partial(far_kernel, k),
            out_shape=acc_shape,
            in_specs=[SMEM, VMEM, VMEM, VMEM],
            out_specs=VMEM,
            input_output_aliases={3: 0},
            compiler_params=small,
            cost_estimate=cost(1),
        )(table, buffer, chunks[k], acc)
    _, halves, *pieces = pl.pallas_call(
        functools.partial(last_kernel, aux_size - 1),
        out_shape=[acc_shape, halves_shape] + [piece_shape] * (occ_size - 1),
        in_specs=[SMEM, VMEM, VMEM, VMEM],
        out_specs=[VMEM] * (occ_size + 1),
        input_output_aliases={3: 0},
        compiler_params=small,
        cost_estimate=cost(1),
        name="last",
    )(table, buffer, chunks[aux_size - 1], acc)
    kept = pl.pallas_call(
        functools.partial(share_kernel, 0),
        out_shape=piece_shape,
        in_specs=[VMEM],
        out_specs=VMEM,
        compiler_params=small,
        cost_estimate=cost(1),
        name="kept",
    )(halves)

    terms = [kept] + [
        lax.ppermute(pieces[k - 1], "occ", exchange_pairs(k, occ_size)) for k in range(1, occ_size)
    ]
    rows = width // aux_size
    mine = pl.pallas_call(
        split_kernel,
        out_shape=[jax.ShapeDtypeStruct((rows, share), jnp.float32)] * aux_size,
        in_specs=[VMEM] * occ_size,
        out_specs=[VMEM] * aux_size,
        compiler_params=pltpu.CompilerParams(vmem_limit_bytes=8 << 20),
        name="split",
    )(*terms)
    total = mine[0]
    for k in range(1, aux_size):
        total = total + lax.ppermute(mine[k], "aux", exchange_pairs(k, aux_size))
    total = total / (columns * occ_size)
    shares = [total] + [
        lax.ppermute(total, "occ", exchange_pairs(k, occ_size)) for k in range(1, occ_size)
    ]
    ordered = []
    for o in range(occ_size):
        value = shares[0]
        for k in range(1, occ_size):
            value = jnp.where((my_occ ^ k) == o, shares[k], value)
        ordered.append(value)
    return jnp.concatenate(ordered, 1)[None]


def solution(mesh):
    placed = (P("aux", "blk", None, None, None), P("blk", "occ"), P("blk", None), P("blk"))
    return jax.shard_map(
        per_device, mesh=mesh, in_specs=placed, out_specs=P("blk", "aux", None), check_vma=False
    )
```

```python
import functools
import math

import jax
import jax.numpy as jnp
from jax import lax
from jax.experimental import pallas as pl
from jax.experimental.pallas import tpu as pltpu
from jax.sharding import PartitionSpec as P


ANY = pl.BlockSpec(memory_space=pl.ANY)
VMEM = pl.BlockSpec(memory_space=pltpu.VMEM)
SMEM = pl.BlockSpec(memory_space=pltpu.SMEM)
HBM = pl.BlockSpec(memory_space=pltpu.HBM)


def exchange_pairs(distance, size):
    return [(i, i ^ distance) for i in range(size)]


def in_hbm(x):
    return pltpu.with_memory_space_constraint(x, pltpu.HBM)


def add_slot(table, i, ints_ref, coef, acc_ref):
    aux_total, _, _, width, _ = ints_ref.shape
    left = ints_ref[:, 0, table[i]].reshape(aux_total * width, width)
    product = jnp.dot(left, coef, preferred_element_type=jnp.float32)
    acc_ref[...] += product.reshape(acc_ref.shape)


def head_kernel(piece, t, coef_hbm, out_ref, sem):
    width = coef_hbm.shape[0]
    depth = (lax.axis_size("blk") - 2) * width // lax.axis_size("aux")
    start = lax.rem(lax.axis_index("aux") * depth + t * piece, width)
    rows = pl.ds(pl.multiple_of(start, piece), piece)
    copy = pltpu.make_async_copy(coef_hbm.at[rows], out_ref, sem)
    copy.start()
    copy.wait()


def own_kernel(counts, lists_hbm, ints_ref, coef_hbm, acc_ref, table, coef, lists, sems):
    slot_total = ints_ref.shape[2]
    lists_copy = pltpu.make_async_copy(lists_hbm, lists, sems.at[0])
    lists_copy.start()
    coef_copy = pltpu.make_async_copy(coef_hbm, coef, sems.at[1])
    coef_copy.start()
    acc_ref[...] = jnp.zeros_like(acc_ref)
    lists_copy.wait()
    me = lax.axis_index("blk")
    live = counts[0]
    found = jnp.int32(0)
    for step, (lo, hi) in enumerate(((0, 1), (1, 2), (2, 1 << 30))):
        for slot in range(slot_total):
            away = lists[0, slot] ^ me
            table[found] = slot
            table[slot_total + 1 + found] = away
            found = found + ((slot < live) & (away >= lo) & (away < hi)).astype(jnp.int32)
        table[2 * slot_total + 2 + step] = found
    coef_copy.wait()

    @pl.loop(0, table[2 * slot_total + 2])
    def _(i):
        add_slot(table, i, ints_ref, coef[...], acc_ref)


def next_kernel(table, ints_ref, next_ref, _acc, acc_ref):
    slot_total = ints_ref.shape[2]

    @pl.loop(table[2 * slot_total + 2], table[2 * slot_total + 3])
    def _(i):
        add_slot(table, i, ints_ref, next_ref[...], acc_ref)


def add_far(distances, complete_after, table, ints_ref, chunks, coef, acc_ref):
    _, _, slot_total, width, _ = ints_ref.shape
    depth = chunks[0].shape[0]
    piece = math.gcd(depth, width)
    me = lax.axis_index("aux")
    for k, chunk in enumerate(chunks):
        if k in complete_after:
            rows = pl.ds(pl.multiple_of((me ^ k) * depth, depth), depth)
            coef[rows, :] = chunk[...]

    @pl.loop(table[2 * slot_total + 3], table[2 * slot_total + 4])
    def _(i):
        start = (table[slot_total + 1 + i] - 2) * width
        last = jnp.int32(0)
        for part in range(width // piece):
            last = jnp.maximum(last, ((start + part * piece) // depth) ^ me)

        @pl.when((last >= distances[0]) & (last <= distances[-1]))
        def _():
            rows = pl.ds(pl.multiple_of(start, width), width)
            add_slot(table, i, ints_ref, coef[rows, :], acc_ref)


def far_kernel(distances, needed, table, ints_ref, *rest):
    *chunks, _, acc_ref, coef = rest
    add_far(distances, needed, table, ints_ref, chunks, coef, acc_ref)


def last_kernel(distances, needed, occ_size, table, ints_ref, *rest):
    *chunks, _, acc_ref, halves = rest[: -occ_size]
    pieces, coef = rest[-occ_size:-1], rest[-1]
    add_far(distances, needed, table, ints_ref, chunks, coef, acc_ref)
    columns = acc_ref.shape[2]
    for p in range(acc_ref.shape[0]):
        halves[:, p * columns : (p + 1) * columns] = acc_ref[p].astype(jnp.bfloat16)
    for k, piece_ref in enumerate(pieces, 1):
        share_kernel(k, halves, piece_ref)


def share_kernel(distance, halves, piece_ref):
    share = piece_ref.shape[1]
    start = (lax.axis_index("occ") ^ distance) * share
    rows = pl.ds(pl.multiple_of(start, share), share)
    piece_ref[...] = lax.dot_general(
        halves[...], halves[rows, :], (((1,), (1,)), ((), ())), preferred_element_type=jnp.float32
    )


def split_kernel(*refs):
    aux_size, occ_size = lax.axis_size("aux"), lax.axis_size("occ")
    terms, outs = refs[:occ_size], refs[occ_size:]
    my_aux = lax.axis_index("aux")
    depth = outs[0].shape[0]
    for k in range(aux_size):
        rows = pl.ds(pl.multiple_of((my_aux ^ k) * depth, depth), depth)
        total = terms[0][rows, :]
        for term in terms[1:]:
            total = total + term[rows, :]
        outs[k][...] = total


def per_device(integrals, orbitals, pair_lists, pair_counts):
    aux_total, _, slot_total, width, _ = integrals.shape
    columns = orbitals.shape[1]
    aux_size, blk_size, occ_size = (lax.axis_size(n) for n in ("aux", "blk", "occ"))
    my_occ = lax.axis_index("occ")
    slot_flops = 2 * aux_total * width * width * columns
    slot_bytes = 2 * aux_total * width * width

    def cost(slots):
        return pl.CostEstimate(
            flops=slots * slot_flops, bytes_accessed=slots * slot_bytes, transcendentals=0
        )

    depth = (blk_size - 2) * width // aux_size
    piece = math.gcd(depth, width)
    parts = []
    for t in range(depth // piece):
        starts = [a * depth + t * piece for a in range(aux_size)]
        pairs = [
            (a * blk_size + i, a * blk_size + (i ^ (2 + starts[a] // width)))
            for a in range(aux_size)
            for i in range(blk_size)
        ]
        sent = pl.pallas_call(
            functools.partial(head_kernel, piece, t),
            out_shape=jax.ShapeDtypeStruct((piece, columns), orbitals.dtype),
            in_specs=[HBM],
            out_specs=VMEM,
            scratch_shapes=[pltpu.SemaphoreType.DMA],
            compiler_params=pltpu.CompilerParams(vmem_limit_bytes=1 << 20),
            cost_estimate=cost(8 * slot_total),
            name="head",
        )(in_hbm(orbitals))
        parts.append(lax.ppermute(sent, ("aux", "blk"), pairs))
    next_block = lax.ppermute(orbitals, "blk", exchange_pairs(1, blk_size))
    chunk = parts[0] if len(parts) == 1 else jnp.concatenate(parts, 0)
    chunks = [chunk] + [
        lax.ppermute(chunk, "aux", exchange_pairs(k, aux_size)) for k in range(1, aux_size)
    ]

    acc_shape = jax.ShapeDtypeStruct((aux_total, width, columns), jnp.float32)
    table_shape = jax.ShapeDtypeStruct((2 * slot_total + 5,), jnp.int32)
    small = pltpu.CompilerParams(vmem_limit_bytes=8 << 20)
    ints = integrals

    acc, table = pl.pallas_call(
        own_kernel,
        out_shape=(acc_shape, table_shape),
        in_specs=[SMEM, HBM, VMEM, HBM],
        out_specs=(VMEM, SMEM),
        scratch_shapes=[
            pltpu.VMEM((width, columns), jnp.bfloat16),
            pltpu.SMEM(pair_lists.shape, jnp.int32),
            pltpu.SemaphoreType.DMA((2,)),
        ],
        compiler_params=small,
        cost_estimate=cost(3),
        name="own",
    )(pair_counts, in_hbm(pair_lists), ints, in_hbm(orbitals))
    acc = pl.pallas_call(
        next_kernel,
        out_shape=acc_shape,
        in_specs=[SMEM, VMEM, VMEM, VMEM],
        out_specs=VMEM,
        input_output_aliases={3: 0},
        compiler_params=small,
        cost_estimate=cost(3),
        name="next",
    )(table, ints, next_block, acc)

    share = width // occ_size
    piece_shape = jax.ShapeDtypeStruct((width, share), jnp.float32)
    halves_shape = jax.ShapeDtypeStruct((width, aux_total * columns), jnp.bfloat16)
    far_scratch = [pltpu.VMEM((aux_size * depth, columns), jnp.bfloat16)]
    far_params = pltpu.CompilerParams(
        vmem_limit_bytes=(6 << 20) + 2 * columns * depth * aux_size
    )
    whole_pairs = (2 * depth) % width == 0
    acc = pl.pallas_call(
        functools.partial(far_kernel, (0, 1), (0, 1)),
        out_shape=acc_shape,
        in_specs=[SMEM] + [VMEM] * 4,
        out_specs=VMEM,
        scratch_shapes=far_scratch,
        input_output_aliases={4: 0},
        compiler_params=far_params,
        cost_estimate=cost(3),
        name="far",
    )(table, ints, *chunks[:2], acc)
    needed = tuple(range(2 if whole_pairs else 0, aux_size))
    _, halves, *pieces = pl.pallas_call(
        functools.partial(last_kernel, (2, aux_size - 1), needed, occ_size),
        out_shape=[acc_shape, halves_shape] + [piece_shape] * (occ_size - 1),
        in_specs=[SMEM, VMEM] + [VMEM] * (aux_size + 1),
        out_specs=[VMEM] * (occ_size + 1),
        scratch_shapes=far_scratch,
        input_output_aliases={aux_size + 2: 0},
        compiler_params=far_params,
        cost_estimate=cost(3),
        name="last",
    )(table, ints, *chunks, acc)
    kept = pl.pallas_call(
        functools.partial(share_kernel, 0),
        out_shape=piece_shape,
        in_specs=[VMEM],
        out_specs=VMEM,
        compiler_params=small,
        cost_estimate=cost(1),
        name="kept",
    )(halves)

    terms = [kept] + [
        lax.ppermute(pieces[k - 1], "occ", exchange_pairs(k, occ_size)) for k in range(1, occ_size)
    ]
    rows = width // aux_size
    mine = pl.pallas_call(
        split_kernel,
        out_shape=[jax.ShapeDtypeStruct((rows, share), jnp.float32)] * aux_size,
        in_specs=[VMEM] * occ_size,
        out_specs=[VMEM] * aux_size,
        compiler_params=pltpu.CompilerParams(vmem_limit_bytes=8 << 20),
        name="split",
    )(*terms)
    total = mine[0]
    for k in range(1, aux_size):
        total = total + lax.ppermute(mine[k], "aux", exchange_pairs(k, aux_size))
    total = total / (columns * occ_size)
    shares = [total] + [
        lax.ppermute(total, "occ", exchange_pairs(k, occ_size)) for k in range(1, occ_size)
    ]
    ordered = []
    for o in range(occ_size):
        value = shares[0]
        for k in range(1, occ_size):
            value = jnp.where((my_occ ^ k) == o, shares[k], value)
        ordered.append(value)
    return jnp.concatenate(ordered, 1)[None]


def solution(mesh):
    placed = (P("aux", "blk", None, None, None), P("blk", "occ"), P("blk", None), P("blk"))
    return jax.shard_map(
        per_device, mesh=mesh, in_specs=placed, out_specs=P("blk", "aux", None), check_vma=False
    )
```

```python
import functools
import math

import jax
import jax.numpy as jnp
from jax import lax
from jax.experimental import pallas as pl
from jax.experimental.pallas import tpu as pltpu
from jax.sharding import PartitionSpec as P


ANY = pl.BlockSpec(memory_space=pl.ANY)
VMEM = pl.BlockSpec(memory_space=pltpu.VMEM)
SMEM = pl.BlockSpec(memory_space=pltpu.SMEM)
HBM = pl.BlockSpec(memory_space=pltpu.HBM)


SCALED_TOP = 14
EXPONENT_ROWS = 16


def exchange_pairs(distance, size):
    return [(i, i ^ distance) for i in range(size)]


def in_hbm(x):
    return pltpu.with_memory_space_constraint(x, pltpu.HBM)


def slot_product(block, coef):
    aux_total, width, _ = block.shape
    product = jnp.dot(
        block.reshape(aux_total * width, width), coef, preferred_element_type=jnp.float32
    )
    return product.reshape(aux_total, width, coef.shape[1])


def add_slot(table, i, ints_ref, coef, acc_ref):
    acc_ref[...] += slot_product(ints_ref[:, 0, table[i]], coef)


def head_kernel(piece, t, coef_hbm, out_ref, sem):
    width = coef_hbm.shape[0]
    depth = (lax.axis_size("blk") - 2) * width // lax.axis_size("aux")
    start = lax.rem(lax.axis_index("aux") * depth + t * piece, width)
    rows = pl.ds(pl.multiple_of(start, piece), piece)
    copy = pltpu.make_async_copy(coef_hbm.at[rows], out_ref, sem)
    copy.start()
    copy.wait()


def first_kernel(counts, lists_hbm, ints_hbm, coef, acc_ref, table, lists, buffer, sems):
    slot_total = ints_hbm.shape[2]
    lists_copy = pltpu.make_async_copy(lists_hbm, lists, sems.at[0])
    slot_copy = pltpu.make_async_copy(ints_hbm.at[:, 0, 0], buffer, sems.at[1])
    lists_copy.start()
    slot_copy.start()
    lists_copy.wait()
    me = lax.axis_index("blk")
    live = counts[0]
    found = jnp.int32(0)
    for step, (lo, hi) in enumerate(((0, 1), (1, 2), (2, 1 << 30))):
        for slot in range(slot_total):
            away = lists[0, slot] ^ me
            table[found] = slot
            table[slot_total + 1 + found] = away
            found = found + ((slot < live) & (away >= lo) & (away < hi)).astype(jnp.int32)
        table[2 * slot_total + 2 + step] = found
    slot_copy.wait()
    acc_ref[...] = slot_product(buffer[...], coef[...])


def near_kernel(distance, table, ints_ref, coef_ref, _acc, acc_ref):
    ends = 2 * ints_ref.shape[2] + 2

    @pl.loop(table[ends + distance - 1] if distance else 1, table[ends + distance])
    def _(i):
        add_slot(table, i, ints_ref, coef_ref[...], acc_ref)


def add_far(distances, complete_after, table, ints_ref, chunks, coef, acc_ref):
    _, _, slot_total, width, _ = ints_ref.shape
    depth = chunks[0].shape[0]
    piece = math.gcd(depth, width)
    me = lax.axis_index("aux")
    for k, chunk in enumerate(chunks):
        if k in complete_after:
            rows = pl.ds(pl.multiple_of((me ^ k) * depth, depth), depth)
            coef[rows, :] = chunk[...]

    @pl.loop(table[2 * slot_total + 3], table[2 * slot_total + 4])
    def _(i):
        start = (table[slot_total + 1 + i] - 2) * width
        last = jnp.int32(0)
        for part in range(width // piece):
            last = jnp.maximum(last, ((start + part * piece) // depth) ^ me)

        @pl.when((last >= distances[0]) & (last <= distances[-1]))
        def _():
            rows = pl.ds(pl.multiple_of(start, width), width)
            add_slot(table, i, ints_ref, coef[rows, :], acc_ref)


def far_kernel(distances, needed, table, ints_ref, *rest):
    *chunks, _, acc_ref, coef = rest
    add_far(distances, needed, table, ints_ref, chunks, coef, acc_ref)


def last_kernel(distances, needed, occ_size, table, ints_ref, *rest):
    *chunks, _, acc_ref, halves = rest[: -occ_size]
    pieces, coef = rest[-occ_size:-1], rest[-1]
    add_far(distances, needed, table, ints_ref, chunks, coef, acc_ref)
    columns = acc_ref.shape[2]
    for p in range(acc_ref.shape[0]):
        halves[:, p * columns : (p + 1) * columns] = acc_ref[p].astype(jnp.bfloat16)
    for k, piece_ref in enumerate(pieces, 1):
        share_kernel(k, halves, piece_ref)


def share_kernel(distance, halves, piece_ref):
    share = piece_ref.shape[1]
    start = (lax.axis_index("occ") ^ distance) * share
    rows = pl.ds(pl.multiple_of(start, share), share)
    piece_ref[...] = lax.dot_general(
        halves[...], halves[rows, :], (((1,), (1,)), ((), ())), preferred_element_type=jnp.float32
    )


def split_kernel(*refs):
    aux_size, occ_size = lax.axis_size("aux"), lax.axis_size("occ")
    terms, outs = refs[:occ_size], refs[occ_size:]
    my_aux = lax.axis_index("aux")
    depth = outs[0].shape[0]
    for k in range(aux_size):
        rows = pl.ds(pl.multiple_of((my_aux ^ k) * depth, depth), depth)
        total = terms[0][rows, :]
        for term in terms[1:]:
            total = total + term[rows, :]
        if k == 0:
            outs[k][...] = total
            continue
        peak = jnp.max(jnp.abs(total), axis=0, keepdims=True)
        exponent = jnp.ceil(jnp.log(jnp.maximum(peak, 2.0**-100)) * (1 / math.log(2.0)))
        outs[k][:depth, :] = total * jnp.exp2(SCALED_TOP - exponent)
        outs[k][depth:, :] = jnp.broadcast_to(exponent, (EXPONENT_ROWS, total.shape[1]))


def unscaled(block, depth):
    block = block.astype(jnp.float32)
    return block[:depth] * jnp.exp2(block[depth : depth + 1] - SCALED_TOP)


def per_device(integrals, orbitals, pair_lists, pair_counts):
    aux_total, _, slot_total, width, _ = integrals.shape
    columns = orbitals.shape[1]
    aux_size, blk_size, occ_size = (lax.axis_size(n) for n in ("aux", "blk", "occ"))
    my_occ = lax.axis_index("occ")
    slot_flops = 2 * aux_total * width * width * columns
    slot_bytes = 2 * aux_total * width * width

    def cost(slots):
        return pl.CostEstimate(
            flops=slots * slot_flops, bytes_accessed=slots * slot_bytes, transcendentals=0
        )

    depth = (blk_size - 2) * width // aux_size
    piece = math.gcd(depth, width)
    parts = []
    for t in range(depth // piece):
        starts = [a * depth + t * piece for a in range(aux_size)]
        pairs = [
            (a * blk_size + i, a * blk_size + (i ^ (2 + starts[a] // width)))
            for a in range(aux_size)
            for i in range(blk_size)
        ]
        sent = pl.pallas_call(
            functools.partial(head_kernel, piece, t),
            out_shape=jax.ShapeDtypeStruct((piece, columns), orbitals.dtype),
            in_specs=[HBM],
            out_specs=VMEM,
            scratch_shapes=[pltpu.SemaphoreType.DMA],
            compiler_params=pltpu.CompilerParams(vmem_limit_bytes=1 << 20),
            cost_estimate=cost(4 * slot_total),
            name="head",
        )(in_hbm(orbitals))
        parts.append(lax.ppermute(sent, ("aux", "blk"), pairs))
    next_block = lax.ppermute(orbitals, "blk", exchange_pairs(1, blk_size))
    chunk = parts[0] if len(parts) == 1 else jnp.concatenate(parts, 0)

    acc_shape = jax.ShapeDtypeStruct((aux_total, width, columns), jnp.float32)
    table_shape = jax.ShapeDtypeStruct((2 * slot_total + 5,), jnp.int32)
    small = pltpu.CompilerParams(vmem_limit_bytes=8 << 20)
    ints = integrals

    acc, table = pl.pallas_call(
        first_kernel,
        out_shape=(acc_shape, table_shape),
        in_specs=[SMEM, HBM, HBM, VMEM],
        out_specs=(VMEM, SMEM),
        scratch_shapes=[
            pltpu.SMEM(pair_lists.shape, jnp.int32),
            pltpu.VMEM((aux_total, width, width), jnp.bfloat16),
            pltpu.SemaphoreType.DMA((2,)),
        ],
        compiler_params=pltpu.CompilerParams(vmem_limit_bytes=(6 << 20) + slot_bytes),
        cost_estimate=cost(1),
        name="first",
    )(pair_counts, in_hbm(pair_lists), in_hbm(integrals), orbitals)

    def near(distance, coef, acc):
        return pl.pallas_call(
            functools.partial(near_kernel, distance),
            out_shape=acc_shape,
            in_specs=[SMEM, VMEM, VMEM, VMEM],
            out_specs=VMEM,
            input_output_aliases={3: 0},
            compiler_params=small,
            cost_estimate=cost(2),
        )(table, ints, coef, acc)

    acc = near(0, orbitals, acc)
    chunk, acc = lax.optimization_barrier((chunk, acc))
    chunks = [chunk] + [
        lax.ppermute(chunk, "aux", exchange_pairs(k, aux_size)) for k in range(1, aux_size)
    ]
    acc = near(1, next_block, acc)

    share = width // occ_size
    piece_shape = jax.ShapeDtypeStruct((width, share), jnp.float32)
    halves_shape = jax.ShapeDtypeStruct((width, aux_total * columns), jnp.bfloat16)
    far_scratch = [pltpu.VMEM((aux_size * depth, columns), jnp.bfloat16)]
    far_params = pltpu.CompilerParams(
        vmem_limit_bytes=(6 << 20) + 2 * columns * depth * aux_size
    )
    whole_pairs = (2 * depth) % width == 0
    acc = pl.pallas_call(
        functools.partial(far_kernel, (0, 1), (0, 1)),
        out_shape=acc_shape,
        in_specs=[SMEM] + [VMEM] * 4,
        out_specs=VMEM,
        scratch_shapes=far_scratch,
        input_output_aliases={4: 0},
        compiler_params=far_params,
        cost_estimate=cost(3),
        name="far",
    )(table, ints, *chunks[:2], acc)
    needed = tuple(range(2 if whole_pairs else 0, aux_size))
    _, halves, *pieces = pl.pallas_call(
        functools.partial(last_kernel, (2, aux_size - 1), needed, occ_size),
        out_shape=[acc_shape, halves_shape] + [piece_shape] * (occ_size - 1),
        in_specs=[SMEM, VMEM] + [VMEM] * (aux_size + 1),
        out_specs=[VMEM] * (occ_size + 1),
        scratch_shapes=far_scratch,
        input_output_aliases={aux_size + 2: 0},
        compiler_params=far_params,
        cost_estimate=cost(3),
        name="last",
    )(table, ints, *chunks, acc)
    kept = pl.pallas_call(
        functools.partial(share_kernel, 0),
        out_shape=piece_shape,
        in_specs=[VMEM],
        out_specs=VMEM,
        compiler_params=small,
        cost_estimate=cost(1),
        name="kept",
    )(halves)

    terms = [kept] + [
        lax.ppermute(pieces[k - 1], "occ", exchange_pairs(k, occ_size)) for k in range(1, occ_size)
    ]
    rows = width // aux_size
    mine = pl.pallas_call(
        split_kernel,
        out_shape=[jax.ShapeDtypeStruct((rows, share), jnp.float32)]
        + [jax.ShapeDtypeStruct((rows + EXPONENT_ROWS, share), jnp.float32)] * (aux_size - 1),
        in_specs=[VMEM] * occ_size,
        out_specs=[VMEM] * aux_size,
        compiler_params=pltpu.CompilerParams(vmem_limit_bytes=8 << 20),
        name="split",
    )(*terms)
    total = mine[0]
    for k in range(1, aux_size):
        sent = mine[k].astype(jnp.float16)
        total = total + unscaled(lax.ppermute(sent, "aux", exchange_pairs(k, aux_size)), rows)
    total = total / (columns * occ_size)
    shares = [total] + [
        lax.ppermute(total, "occ", exchange_pairs(k, occ_size)) for k in range(1, occ_size)
    ]
    ordered = []
    for o in range(occ_size):
        value = shares[0]
        for k in range(1, occ_size):
            value = jnp.where((my_occ ^ k) == o, shares[k], value)
        ordered.append(value)
    return jnp.concatenate(ordered, 1)[None]


def solution(mesh):
    placed = (P("aux", "blk", None, None, None), P("blk", "occ"), P("blk", None), P("blk"))
    return jax.shard_map(
        per_device, mesh=mesh, in_specs=placed, out_specs=P("blk", "aux", None), check_vma=False
    )
```

```python
import functools
import math

import jax
import jax.numpy as jnp
from jax import lax
from jax.experimental import pallas as pl
from jax.experimental.pallas import tpu as pltpu
from jax.sharding import PartitionSpec as P


ANY = pl.BlockSpec(memory_space=pl.ANY)
VMEM = pl.BlockSpec(memory_space=pltpu.VMEM)
SMEM = pl.BlockSpec(memory_space=pltpu.SMEM)
HBM = pl.BlockSpec(memory_space=pltpu.HBM)


SCALED_TOP = 14
EXPONENT_ROWS = 16


def exchange_pairs(distance, size):
    return [(i, i ^ distance) for i in range(size)]


def in_hbm(x):
    return pltpu.with_memory_space_constraint(x, pltpu.HBM)


def slot_product(block, coef):
    aux_total, width, _ = block.shape
    product = jnp.dot(
        block.reshape(aux_total * width, width), coef, preferred_element_type=jnp.float32
    )
    return product.reshape(aux_total, width, coef.shape[1])


def add_slots(table, group, ints_ref, coef_rows, acc_ref, fresh=False):
    begin, end = group_bounds(table, group, ints_ref.shape[2])

    def product(i):
        return slot_product(ints_ref[:, 0, table[i]], coef_rows(i))

    if fresh:
        acc_ref[...] = product(0)
        begin = 1
    pairs = (end - begin) // 2

    @pl.loop(0, pairs)
    def _(pair):
        i = begin + 2 * pair
        acc_ref[...] += product(i) + product(i + 1)

    @pl.when(begin + 2 * pairs < end)
    def _():
        acc_ref[...] += product(end - 1)


def group_bounds(table, group, slot_total):
    ends = 2 * slot_total + 2
    return (table[ends + group - 1] if group else 0), table[ends + group]


def head_kernel(piece, t, coef_hbm, out_ref, sem):
    width = coef_hbm.shape[0]
    depth = (lax.axis_size("blk") - 2) * width // lax.axis_size("aux")
    start = lax.rem(lax.axis_index("aux") * depth + t * piece, width)
    rows = pl.ds(pl.multiple_of(start, piece), piece)
    copy = pltpu.make_async_copy(coef_hbm.at[rows], out_ref, sem)
    copy.start()
    copy.wait()


def sort_kernel(far_depth, width, counts, lists_hbm, table, lists, sem):
    slot_total = lists.shape[1]
    copy = pltpu.make_async_copy(lists_hbm, lists, sem)
    copy.start()
    copy.wait()
    me, my_aux = lax.axis_index("blk"), lax.axis_index("aux")
    live = counts[0]
    piece = math.gcd(far_depth, width)
    groups = []
    for slot in range(slot_total):
        away = lists[0, slot] ^ me
        last = jnp.int32(0)
        for part in range(width // piece):
            last = jnp.maximum(last, lax.div((away - 2) * width + part * piece, far_depth) ^ my_aux)
        far_group = jnp.where(last <= 1, 2, 3)
        groups.append(jnp.where(slot < live, jnp.where(away < 2, away, far_group), 4))
    found = jnp.int32(0)
    for group in range(4):
        for slot in range(slot_total):
            table[found] = slot
            table[slot_total + 1 + found] = lists[0, slot] ^ me
            found = found + (groups[slot] == group).astype(jnp.int32)
        table[2 * slot_total + 2 + group] = found


def near_kernel(group, table, ints_ref, coef_ref, *accs):
    add_slots(table, group, ints_ref, lambda i: coef_ref[...], accs[-1], fresh=group == 0)


def add_far(group, needed, table, ints_ref, chunks, coef, acc_ref):
    _, _, slot_total, width, _ = ints_ref.shape
    depth = chunks[0].shape[0]
    me = lax.axis_index("aux")
    for k in needed:
        rows = pl.ds(pl.multiple_of((me ^ k) * depth, depth), depth)
        coef[rows, :] = chunks[k][...]

    def coef_rows(i):
        start = (table[slot_total + 1 + i] - 2) * width
        return coef[pl.ds(pl.multiple_of(start, width), width), :]

    add_slots(table, group, ints_ref, coef_rows, acc_ref)


def far_kernel(needed, table, ints_ref, *rest):
    *chunks, _, acc_ref, coef = rest
    add_far(2, needed, table, ints_ref, chunks, coef, acc_ref)


def last_kernel(needed, occ_size, table, ints_ref, *rest):
    *chunks, _, acc_ref, halves = rest[: -occ_size]
    pieces, coef = rest[-occ_size:-1], rest[-1]
    add_far(3, needed, table, ints_ref, chunks, coef, acc_ref)
    columns = acc_ref.shape[2]
    for p in range(acc_ref.shape[0]):
        halves[:, p * columns : (p + 1) * columns] = acc_ref[p].astype(jnp.bfloat16)
    for k, piece_ref in enumerate(pieces, 1):
        share_kernel(k, halves, piece_ref)


def share_kernel(distance, halves, piece_ref):
    share = piece_ref.shape[1]
    start = (lax.axis_index("occ") ^ distance) * share
    rows = pl.ds(pl.multiple_of(start, share), share)
    piece_ref[...] = lax.dot_general(
        halves[...], halves[rows, :], (((1,), (1,)), ((), ())), preferred_element_type=jnp.float32
    )


def split_kernel(*refs):
    aux_size, occ_size = lax.axis_size("aux"), lax.axis_size("occ")
    terms, outs = refs[:occ_size], refs[occ_size:]
    my_aux = lax.axis_index("aux")
    depth = outs[0].shape[0]
    for k in range(aux_size):
        rows = pl.ds(pl.multiple_of((my_aux ^ k) * depth, depth), depth)
        total = terms[0][rows, :]
        for term in terms[1:]:
            total = total + term[rows, :]
        if k == 0:
            outs[k][...] = total
            continue
        peak = jnp.max(jnp.abs(total), axis=0, keepdims=True)
        exponent = jnp.ceil(jnp.log(jnp.maximum(peak, 2.0**-100)) * (1 / math.log(2.0)))
        outs[k][:depth, :] = total * jnp.exp2(SCALED_TOP - exponent)
        outs[k][depth:, :] = jnp.broadcast_to(exponent, (EXPONENT_ROWS, total.shape[1]))


def unscaled(block, depth):
    block = block.astype(jnp.float32)
    return block[:depth] * jnp.exp2(block[depth : depth + 1] - SCALED_TOP)


def per_device(integrals, orbitals, pair_lists, pair_counts):
    aux_total, _, slot_total, width, _ = integrals.shape
    columns = orbitals.shape[1]
    aux_size, blk_size, occ_size = (lax.axis_size(n) for n in ("aux", "blk", "occ"))
    my_occ = lax.axis_index("occ")
    slot_flops = 2 * aux_total * width * width * columns
    slot_bytes = 2 * aux_total * width * width

    def cost(slots):
        return pl.CostEstimate(
            flops=slots * slot_flops, bytes_accessed=slots * slot_bytes, transcendentals=0
        )

    depth = (blk_size - 2) * width // aux_size
    piece = math.gcd(depth, width)
    parts = []
    for t in range(depth // piece):
        starts = [a * depth + t * piece for a in range(aux_size)]
        pairs = [
            (a * blk_size + i, a * blk_size + (i ^ (2 + starts[a] // width)))
            for a in range(aux_size)
            for i in range(blk_size)
        ]
        sent = pl.pallas_call(
            functools.partial(head_kernel, piece, t),
            out_shape=jax.ShapeDtypeStruct((piece, columns), orbitals.dtype),
            in_specs=[HBM],
            out_specs=VMEM,
            scratch_shapes=[pltpu.SemaphoreType.DMA],
            compiler_params=pltpu.CompilerParams(vmem_limit_bytes=1 << 20),
            cost_estimate=cost(4 * slot_total),
            name="head",
        )(in_hbm(orbitals))
        parts.append(lax.ppermute(sent, ("aux", "blk"), pairs))
    next_block = lax.ppermute(orbitals, "blk", exchange_pairs(1, blk_size))
    chunk = parts[0] if len(parts) == 1 else jnp.concatenate(parts, 0)

    acc_shape = jax.ShapeDtypeStruct((aux_total, width, columns), jnp.float32)
    table_shape = jax.ShapeDtypeStruct((2 * slot_total + 6,), jnp.int32)
    small = pltpu.CompilerParams(vmem_limit_bytes=10 << 20)
    ints = integrals

    table = pl.pallas_call(
        functools.partial(sort_kernel, depth, width),
        out_shape=table_shape,
        in_specs=[SMEM, HBM],
        out_specs=SMEM,
        scratch_shapes=[pltpu.SMEM(pair_lists.shape, jnp.int32), pltpu.SemaphoreType.DMA],
        compiler_params=pltpu.CompilerParams(vmem_limit_bytes=1 << 20),
        cost_estimate=cost(1),
        name="sort",
    )(pair_counts, in_hbm(pair_lists))

    def near(group, coef, *acc):
        return pl.pallas_call(
            functools.partial(near_kernel, group),
            out_shape=acc_shape,
            in_specs=[SMEM, VMEM, VMEM] + [VMEM] * len(acc),
            out_specs=VMEM,
            input_output_aliases={3: 0} if acc else {},
            compiler_params=small,
            cost_estimate=cost(2),
        )(table, ints, coef, *acc)

    acc = near(0, orbitals)
    chunk, acc = lax.optimization_barrier((chunk, acc))
    chunks = [chunk] + [
        lax.ppermute(chunk, "aux", exchange_pairs(k, aux_size)) for k in range(1, aux_size)
    ]
    acc = near(1, next_block, acc)

    share = width // occ_size
    piece_shape = jax.ShapeDtypeStruct((width, share), jnp.float32)
    halves_shape = jax.ShapeDtypeStruct((width, aux_total * columns), jnp.bfloat16)
    far_scratch = [pltpu.VMEM((aux_size * depth, columns), jnp.bfloat16)]
    far_params = pltpu.CompilerParams(
        vmem_limit_bytes=(10 << 20) + 2 * columns * depth * aux_size
    )
    whole_pairs = (2 * depth) % width == 0
    acc = pl.pallas_call(
        functools.partial(far_kernel, (0, 1)),
        out_shape=acc_shape,
        in_specs=[SMEM] + [VMEM] * 4,
        out_specs=VMEM,
        scratch_shapes=far_scratch,
        input_output_aliases={4: 0},
        compiler_params=far_params,
        cost_estimate=cost(3),
        name="far",
    )(table, ints, *chunks[:2], acc)
    needed = tuple(range(2 if whole_pairs else 0, aux_size))
    _, halves, *pieces = pl.pallas_call(
        functools.partial(last_kernel, needed, occ_size),
        out_shape=[acc_shape, halves_shape] + [piece_shape] * (occ_size - 1),
        in_specs=[SMEM, VMEM] + [VMEM] * (aux_size + 1),
        out_specs=[VMEM] * (occ_size + 1),
        scratch_shapes=far_scratch,
        input_output_aliases={aux_size + 2: 0},
        compiler_params=far_params,
        cost_estimate=cost(3),
        name="last",
    )(table, ints, *chunks, acc)
    kept = pl.pallas_call(
        functools.partial(share_kernel, 0),
        out_shape=piece_shape,
        in_specs=[VMEM],
        out_specs=VMEM,
        compiler_params=small,
        cost_estimate=cost(1),
        name="kept",
    )(halves)

    terms = [kept] + [
        lax.ppermute(pieces[k - 1], "occ", exchange_pairs(k, occ_size)) for k in range(1, occ_size)
    ]
    rows = width // aux_size
    mine = pl.pallas_call(
        split_kernel,
        out_shape=[jax.ShapeDtypeStruct((rows, share), jnp.float32)]
        + [jax.ShapeDtypeStruct((rows + EXPONENT_ROWS, share), jnp.float32)] * (aux_size - 1),
        in_specs=[VMEM] * occ_size,
        out_specs=[VMEM] * aux_size,
        compiler_params=pltpu.CompilerParams(vmem_limit_bytes=8 << 20),
        name="split",
    )(*terms)
    total = mine[0]
    for k in range(1, aux_size):
        sent = mine[k].astype(jnp.float16)
        total = total + unscaled(lax.ppermute(sent, "aux", exchange_pairs(k, aux_size)), rows)
    total = total / (columns * occ_size)
    shares = [total] + [
        lax.ppermute(total, "occ", exchange_pairs(k, occ_size)) for k in range(1, occ_size)
    ]
    ordered = []
    for o in range(occ_size):
        value = shares[0]
        for k in range(1, occ_size):
            value = jnp.where((my_occ ^ k) == o, shares[k], value)
        ordered.append(value)
    return jnp.concatenate(ordered, 1)[None]


def solution(mesh):
    placed = (P("aux", "blk", None, None, None), P("blk", "occ"), P("blk", None), P("blk"))
    return jax.shard_map(
        per_device, mesh=mesh, in_specs=placed, out_specs=P("blk", "aux", None), check_vma=False
    )
```

```python
import functools
import math

import jax
import jax.numpy as jnp
from jax import lax
from jax.experimental import pallas as pl
from jax.experimental.pallas import tpu as pltpu
from jax.sharding import PartitionSpec as P


ANY = pl.BlockSpec(memory_space=pl.ANY)
VMEM = pl.BlockSpec(memory_space=pltpu.VMEM)
SMEM = pl.BlockSpec(memory_space=pltpu.SMEM)
HBM = pl.BlockSpec(memory_space=pltpu.HBM)


SCALED_TOP = 14
EXPONENT_ROWS = 16


def exchange_pairs(distance, size):
    return [(i, i ^ distance) for i in range(size)]


def in_hbm(x):
    return pltpu.with_memory_space_constraint(x, pltpu.HBM)


def slot_product(block, coef):
    aux_total, width, _ = block.shape
    product = jnp.dot(
        block.reshape(aux_total * width, width), coef, preferred_element_type=jnp.float32
    )
    return product.reshape(aux_total, width, coef.shape[1])


def add_slots(table, group, ints_ref, coef_rows, acc_ref, fresh=False):
    begin, end = group_bounds(table, group, ints_ref.shape[2])

    def product(i):
        return slot_product(ints_ref[:, 0, table[i]], coef_rows(i))

    if fresh:
        acc_ref[...] = product(0)
        begin = 1
    pairs = (end - begin) // 2

    @pl.loop(0, pairs)
    def _(pair):
        i = begin + 2 * pair
        acc_ref[...] += product(i) + product(i + 1)

    @pl.when(begin + 2 * pairs < end)
    def _():
        acc_ref[...] += product(end - 1)


def group_bounds(table, group, slot_total):
    ends = 2 * slot_total + 2
    return (table[ends + group - 1] if group else 0), table[ends + group]


def head_kernel(piece, t, flips, coef_hbm, *rest):
    *outs, sems = rest
    width = coef_hbm.shape[0]
    depth = (lax.axis_size("blk") - 2) * width // lax.axis_size("aux")
    copies = []
    for i, flip in enumerate(flips):
        start = lax.rem((lax.axis_index("aux") ^ flip) * depth + t * piece, width)
        rows = pl.ds(pl.multiple_of(start, piece), piece)
        copies.append(pltpu.make_async_copy(coef_hbm.at[rows], outs[i], sems.at[i]))
    for copy in copies:
        copy.start()
    for copy in copies:
        copy.wait()


def sort_kernel(far_depth, width, counts, lists, table):
    slot_total = lists.shape[1]
    me, my_aux = lax.axis_index("blk"), lax.axis_index("aux")
    live = counts[0]
    piece = math.gcd(far_depth, width)
    groups = []
    for slot in range(slot_total):
        away = lists[0, slot] ^ me
        last = jnp.int32(0)
        for part in range(width // piece):
            last = jnp.maximum(last, lax.div((away - 2) * width + part * piece, far_depth) ^ my_aux)
        far_group = jnp.where(last <= 1, 2, 3)
        groups.append(jnp.where(slot < live, jnp.where(away < 2, away, far_group), 4))
    found = jnp.int32(0)
    for group in range(4):
        for slot in range(slot_total):
            table[found] = slot
            table[slot_total + 1 + found] = lists[0, slot] ^ me
            found = found + (groups[slot] == group).astype(jnp.int32)
        table[2 * slot_total + 2 + group] = found


def near_kernel(group, table, ints_ref, coef_ref, *accs):
    add_slots(table, group, ints_ref, lambda i: coef_ref[...], accs[-1], fresh=group == 0)


def add_far(group, needed, table, ints_ref, chunks, coef, acc_ref):
    _, _, slot_total, width, _ = ints_ref.shape
    depth = chunks[0].shape[0]
    me = lax.axis_index("aux")
    for k in needed:
        rows = pl.ds(pl.multiple_of((me ^ k) * depth, depth), depth)
        coef[rows, :] = chunks[k][...]

    def coef_rows(i):
        start = (table[slot_total + 1 + i] - 2) * width
        return coef[pl.ds(pl.multiple_of(start, width), width), :]

    add_slots(table, group, ints_ref, coef_rows, acc_ref)


def far_kernel(needed, table, ints_ref, *rest):
    *chunks, _, acc_ref, coef = rest
    add_far(2, needed, table, ints_ref, chunks, coef, acc_ref)


def last_kernel(needed, occ_size, table, ints_ref, *rest):
    *chunks, _, acc_ref, halves = rest[: -occ_size]
    pieces, coef = rest[-occ_size:-1], rest[-1]
    add_far(3, needed, table, ints_ref, chunks, coef, acc_ref)
    columns = acc_ref.shape[2]
    for p in range(acc_ref.shape[0]):
        halves[:, p * columns : (p + 1) * columns] = acc_ref[p].astype(jnp.bfloat16)
    for k, piece_ref in enumerate(pieces, 1):
        share_kernel(k, halves, piece_ref)


def share_kernel(distance, halves, piece_ref):
    share = piece_ref.shape[1]
    start = (lax.axis_index("occ") ^ distance) * share
    rows = pl.ds(pl.multiple_of(start, share), share)
    piece_ref[...] = lax.dot_general(
        halves[...], halves[rows, :], (((1,), (1,)), ((), ())), preferred_element_type=jnp.float32
    )


def split_kernel(*refs):
    aux_size, occ_size = lax.axis_size("aux"), lax.axis_size("occ")
    terms, outs = refs[:occ_size], refs[occ_size:]
    my_aux = lax.axis_index("aux")
    depth = outs[0].shape[0]
    for k in range(aux_size):
        rows = pl.ds(pl.multiple_of((my_aux ^ k) * depth, depth), depth)
        total = terms[0][rows, :]
        for term in terms[1:]:
            total = total + term[rows, :]
        if k == 0:
            outs[k][...] = total
            continue
        peak = jnp.max(jnp.abs(total), axis=0, keepdims=True)
        exponent = jnp.ceil(jnp.log(jnp.maximum(peak, 2.0**-100)) * (1 / math.log(2.0)))
        outs[k][:depth, :] = total * jnp.exp2(SCALED_TOP - exponent)
        outs[k][depth:, :] = jnp.broadcast_to(exponent, (EXPONENT_ROWS, total.shape[1]))


def unscaled(block, depth):
    block = block.astype(jnp.float32)
    return block[:depth] * jnp.exp2(block[depth : depth + 1] - SCALED_TOP)


def per_device(integrals, orbitals, pair_lists, pair_counts):
    aux_total, _, slot_total, width, _ = integrals.shape
    columns = orbitals.shape[1]
    aux_size, blk_size, occ_size = (lax.axis_size(n) for n in ("aux", "blk", "occ"))
    my_occ = lax.axis_index("occ")
    slot_flops = 2 * aux_total * width * width * columns
    slot_bytes = 2 * aux_total * width * width

    def cost(slots):
        return pl.CostEstimate(
            flops=slots * slot_flops, bytes_accessed=slots * slot_bytes, transcendentals=0
        )

    depth = (blk_size - 2) * width // aux_size
    piece = math.gcd(depth, width)

    flips = (0, aux_size - 1)
    to_send = [
        pl.pallas_call(
            functools.partial(head_kernel, piece, t, flips),
            out_shape=[jax.ShapeDtypeStruct((piece, columns), orbitals.dtype)] * 2,
            in_specs=[HBM],
            out_specs=[VMEM] * 2,
            scratch_shapes=[pltpu.SemaphoreType.DMA((2,))],
            compiler_params=pltpu.CompilerParams(vmem_limit_bytes=1 << 20),
            cost_estimate=cost(16 * slot_total),
            name="head",
        )(in_hbm(orbitals))
        for t in range(depth // piece)
    ]

    def fetch_chunk(flip, rows):
        parts = []
        for t, sent in enumerate(rows):
            starts = [(a ^ flip) * depth + t * piece for a in range(aux_size)]
            pairs = [
                (a * blk_size + i, a * blk_size + (i ^ (2 + starts[a] // width)))
                for a in range(aux_size)
                for i in range(blk_size)
            ]
            parts.append(lax.ppermute(sent, ("aux", "blk"), pairs))
        return parts[0] if len(parts) == 1 else jnp.concatenate(parts, 0)

    chunk = fetch_chunk(flips[0], [rows for rows, _ in to_send])
    next_block = lax.ppermute(orbitals, "blk", exchange_pairs(1, blk_size))

    acc_shape = jax.ShapeDtypeStruct((aux_total, width, columns), jnp.float32)
    table_shape = jax.ShapeDtypeStruct((2 * slot_total + 6,), jnp.int32)
    small = pltpu.CompilerParams(vmem_limit_bytes=10 << 20)
    ints = integrals

    table = pl.pallas_call(
        functools.partial(sort_kernel, depth, width),
        out_shape=table_shape,
        in_specs=[SMEM, SMEM],
        out_specs=SMEM,
        compiler_params=pltpu.CompilerParams(vmem_limit_bytes=1 << 20),
        cost_estimate=cost(1),
        name="sort",
    )(pair_counts, pair_lists)

    def near(group, coef, *acc):
        return pl.pallas_call(
            functools.partial(near_kernel, group),
            out_shape=acc_shape,
            in_specs=[SMEM, VMEM, VMEM] + [VMEM] * len(acc),
            out_specs=VMEM,
            input_output_aliases={3: 0} if acc else {},
            compiler_params=small,
            cost_estimate=cost(2),
        )(table, ints, coef, *acc)

    acc = near(0, orbitals)
    across = [rows for _, rows in to_send]
    chunk, acc, across = lax.optimization_barrier((chunk, acc, across))
    chunks = [chunk] + [
        lax.ppermute(chunk, "aux", exchange_pairs(k, aux_size)) for k in range(1, aux_size - 1)
    ]
    chunks.append(fetch_chunk(flips[1], across))
    acc = near(1, next_block, acc)

    share = width // occ_size
    piece_shape = jax.ShapeDtypeStruct((width, share), jnp.float32)
    halves_shape = jax.ShapeDtypeStruct((width, aux_total * columns), jnp.bfloat16)
    far_scratch = [pltpu.VMEM((aux_size * depth, columns), jnp.bfloat16)]
    far_params = pltpu.CompilerParams(
        vmem_limit_bytes=(10 << 20) + 2 * columns * depth * aux_size
    )
    whole_pairs = (2 * depth) % width == 0
    acc = pl.pallas_call(
        functools.partial(far_kernel, (0, 1)),
        out_shape=acc_shape,
        in_specs=[SMEM] + [VMEM] * 4,
        out_specs=VMEM,
        scratch_shapes=far_scratch,
        input_output_aliases={4: 0},
        compiler_params=far_params,
        cost_estimate=cost(3),
        name="far",
    )(table, ints, *chunks[:2], acc)
    needed = tuple(range(2 if whole_pairs else 0, aux_size))
    _, halves, *pieces = pl.pallas_call(
        functools.partial(last_kernel, needed, occ_size),
        out_shape=[acc_shape, halves_shape] + [piece_shape] * (occ_size - 1),
        in_specs=[SMEM, VMEM] + [VMEM] * (aux_size + 1),
        out_specs=[VMEM] * (occ_size + 1),
        scratch_shapes=far_scratch,
        input_output_aliases={aux_size + 2: 0},
        compiler_params=far_params,
        cost_estimate=cost(3),
        name="last",
    )(table, ints, *chunks, acc)
    kept = pl.pallas_call(
        functools.partial(share_kernel, 0),
        out_shape=piece_shape,
        in_specs=[VMEM],
        out_specs=VMEM,
        compiler_params=small,
        cost_estimate=cost(1),
        name="kept",
    )(halves)

    terms = [kept] + [
        lax.ppermute(pieces[k - 1], "occ", exchange_pairs(k, occ_size)) for k in range(1, occ_size)
    ]
    rows = width // aux_size
    mine = pl.pallas_call(
        split_kernel,
        out_shape=[jax.ShapeDtypeStruct((rows, share), jnp.float32)]
        + [jax.ShapeDtypeStruct((rows + EXPONENT_ROWS, share), jnp.float32)] * (aux_size - 1),
        in_specs=[VMEM] * occ_size,
        out_specs=[VMEM] * aux_size,
        compiler_params=pltpu.CompilerParams(vmem_limit_bytes=8 << 20),
        name="split",
    )(*terms)
    total = mine[0]
    for k in range(1, aux_size):
        sent = mine[k].astype(jnp.float16)
        total = total + unscaled(lax.ppermute(sent, "aux", exchange_pairs(k, aux_size)), rows)
    total = total / (columns * occ_size)
    shares = [total] + [
        lax.ppermute(total, "occ", exchange_pairs(k, occ_size)) for k in range(1, occ_size)
    ]
    ordered = []
    for o in range(occ_size):
        value = shares[0]
        for k in range(1, occ_size):
            value = jnp.where((my_occ ^ k) == o, shares[k], value)
        ordered.append(value)
    return jnp.concatenate(ordered, 1)[None]


def solution(mesh):
    placed = (P("aux", "blk", None, None, None), P("blk", "occ"), P("blk", None), P("blk"))
    return jax.shard_map(
        per_device, mesh=mesh, in_specs=placed, out_specs=P("blk", "aux", None), check_vma=False
    )
```

```python
import functools
import math

import jax
import jax.numpy as jnp
from jax import lax
from jax.experimental import pallas as pl
from jax.experimental.pallas import tpu as pltpu
from jax.sharding import PartitionSpec as P


ANY = pl.BlockSpec(memory_space=pl.ANY)
VMEM = pl.BlockSpec(memory_space=pltpu.VMEM)
SMEM = pl.BlockSpec(memory_space=pltpu.SMEM)
HBM = pl.BlockSpec(memory_space=pltpu.HBM)


SCALED_TOP = 14
EXPONENT_ROWS = 16


def exchange_pairs(distance, size):
    return [(i, i ^ distance) for i in range(size)]


def mirrored(value, size, core):
    bits = size.bit_length() - 1
    other = sum(((value >> i) & 1) << (bits - 1 - i) for i in range(bits))
    if isinstance(core, int):
        return other if core % 2 else value
    return jnp.where(core % 2 == 1, other, value)


def my_seat():
    return mirrored(lax.axis_index("aux"), lax.axis_size("aux"), lax.axis_index("occ"))


def aux_exchange(distance, aux_size, occ_size):
    return [
        (a * occ_size + c, (a ^ mirrored(distance, aux_size, c)) * occ_size + c)
        for a in range(aux_size)
        for c in range(occ_size)
    ]


def in_hbm(x):
    return pltpu.with_memory_space_constraint(x, pltpu.HBM)


def slot_product(block, coef):
    aux_total, width, _ = block.shape
    product = jnp.dot(
        block.reshape(aux_total * width, width), coef, preferred_element_type=jnp.float32
    )
    return product.reshape(aux_total, width, coef.shape[1])


def add_slots(table, group, ints_ref, coef_rows, acc_ref, fresh=False):
    begin, end = group_bounds(table, group, ints_ref.shape[2])

    def product(i):
        return slot_product(ints_ref[:, 0, table[i]], coef_rows(i))

    if fresh:
        acc_ref[...] = product(0)
        begin = 1
    pairs = (end - begin) // 2

    @pl.loop(0, pairs)
    def _(pair):
        i = begin + 2 * pair
        acc_ref[...] += product(i) + product(i + 1)

    @pl.when(begin + 2 * pairs < end)
    def _():
        acc_ref[...] += product(end - 1)


def group_bounds(table, group, slot_total):
    ends = 2 * slot_total + 2
    return (table[ends + group - 1] if group else 0), table[ends + group]


def head_kernel(piece, t, coef_hbm, out_ref, sem):
    width = coef_hbm.shape[0]
    depth = (lax.axis_size("blk") - 2) * width // lax.axis_size("aux")
    start = lax.rem(my_seat() * depth + t * piece, width)
    rows = pl.ds(pl.multiple_of(start, piece), piece)
    copy = pltpu.make_async_copy(coef_hbm.at[rows], out_ref, sem)
    copy.start()
    copy.wait()


def sort_kernel(far_depth, width, counts, lists, table):
    slot_total = lists.shape[1]
    me, seat = lax.axis_index("blk"), my_seat()
    live = counts[0]
    piece = math.gcd(far_depth, width)
    groups, sizes = [], [jnp.int32(0)] * 4
    for slot in range(slot_total):
        away = lists[0, slot] ^ me
        last = jnp.int32(0)
        for part in range(width // piece):
            last = jnp.maximum(last, lax.div((away - 2) * width + part * piece, far_depth) ^ seat)
        far_group = jnp.where(last <= 1, 2, 3)
        groups.append(jnp.where(slot < live, jnp.where(away < 2, away, far_group), 4))
        sizes = [n + (groups[-1] == g).astype(jnp.int32) for g, n in enumerate(sizes)]
    cursors, found = [], jnp.int32(0)
    for group, size in enumerate(sizes):
        cursors.append(found)
        found = found + size
        table[2 * slot_total + 2 + group] = found
    for slot in range(slot_total):
        place = jnp.int32(slot_total)
        for group in range(4):
            place = jnp.where(groups[slot] == group, cursors[group], place)
        cursors = [n + (groups[slot] == g).astype(jnp.int32) for g, n in enumerate(cursors)]
        table[place] = slot
        table[slot_total + 1 + place] = lists[0, slot] ^ me


def near_kernel(group, table, ints_ref, coef_ref, *accs):
    add_slots(table, group, ints_ref, lambda i: coef_ref[...], accs[-1], fresh=group == 0)


def add_far(group, needed, table, ints_ref, chunks, coef, acc_ref):
    _, _, slot_total, width, _ = ints_ref.shape
    depth = chunks[0].shape[0]
    me = my_seat()
    for k in needed:
        rows = pl.ds(pl.multiple_of((me ^ k) * depth, depth), depth)
        coef[rows, :] = chunks[k][...]

    def coef_rows(i):
        start = (table[slot_total + 1 + i] - 2) * width
        return coef[pl.ds(pl.multiple_of(start, width), width), :]

    add_slots(table, group, ints_ref, coef_rows, acc_ref)


def far_kernel(needed, table, ints_ref, *rest):
    *chunks, _, acc_ref, coef = rest
    add_far(2, needed, table, ints_ref, chunks, coef, acc_ref)


def last_kernel(needed, occ_size, table, ints_ref, *rest):
    *chunks, _, acc_ref, halves = rest[: -occ_size]
    pieces, coef = rest[-occ_size:-1], rest[-1]
    add_far(3, needed, table, ints_ref, chunks, coef, acc_ref)
    columns = acc_ref.shape[2]
    for p in range(acc_ref.shape[0]):
        halves[:, p * columns : (p + 1) * columns] = acc_ref[p].astype(jnp.bfloat16)
    for k, piece_ref in enumerate(pieces, 1):
        share_kernel(k, halves, piece_ref)


def share_kernel(distance, halves, piece_ref):
    share = piece_ref.shape[1]
    start = (lax.axis_index("occ") ^ distance) * share
    rows = pl.ds(pl.multiple_of(start, share), share)
    piece_ref[...] = lax.dot_general(
        halves[...], halves[rows, :], (((1,), (1,)), ((), ())), preferred_element_type=jnp.float32
    )


def split_kernel(*refs):
    aux_size, occ_size = lax.axis_size("aux"), lax.axis_size("occ")
    terms, outs = refs[:occ_size], refs[occ_size:]
    my_aux, my_occ = lax.axis_index("aux"), lax.axis_index("occ")
    depth = outs[0].shape[0]
    for k in range(aux_size):
        target = my_aux ^ mirrored(k, aux_size, my_occ)
        rows = pl.ds(pl.multiple_of(target * depth, depth), depth)
        total = terms[0][rows, :]
        for term in terms[1:]:
            total = total + term[rows, :]
        if k == 0:
            outs[k][...] = total
            continue
        peak = jnp.max(jnp.abs(total), axis=0, keepdims=True)
        exponent = jnp.ceil(jnp.log(jnp.maximum(peak, 2.0**-100)) * (1 / math.log(2.0)))
        outs[k][:depth, :] = total * jnp.exp2(SCALED_TOP - exponent)
        outs[k][depth:, :] = jnp.broadcast_to(exponent, (EXPONENT_ROWS, total.shape[1]))


def unscaled(block, depth):
    block = block.astype(jnp.float32)
    return block[:depth] * jnp.exp2(block[depth : depth + 1] - SCALED_TOP)


def per_device(integrals, orbitals, pair_lists, pair_counts):
    aux_total, _, slot_total, width, _ = integrals.shape
    columns = orbitals.shape[1]
    aux_size, blk_size, occ_size = (lax.axis_size(n) for n in ("aux", "blk", "occ"))
    my_occ = lax.axis_index("occ")
    slot_flops = 2 * aux_total * width * width * columns
    slot_bytes = 2 * aux_total * width * width

    def cost(slots):
        return pl.CostEstimate(
            flops=slots * slot_flops, bytes_accessed=slots * slot_bytes, transcendentals=0
        )

    depth = (blk_size - 2) * width // aux_size
    piece = math.gcd(depth, width)
    parts = []
    for t in range(depth // piece):
        pairs = []
        for a in range(aux_size):
            for c in range(occ_size):
                away = 2 + (mirrored(a, aux_size, c) * depth + t * piece) // width
                pairs += [
                    ((a * blk_size + i) * occ_size + c, (a * blk_size + (i ^ away)) * occ_size + c)
                    for i in range(blk_size)
                ]
        sent = pl.pallas_call(
            functools.partial(head_kernel, piece, t),
            out_shape=jax.ShapeDtypeStruct((piece, columns), orbitals.dtype),
            in_specs=[HBM],
            out_specs=VMEM,
            scratch_shapes=[pltpu.SemaphoreType.DMA],
            compiler_params=pltpu.CompilerParams(vmem_limit_bytes=1 << 20),
            cost_estimate=cost(4 * slot_total),
            name="head",
        )(in_hbm(orbitals))
        parts.append(lax.ppermute(sent, ("aux", "blk", "occ"), pairs))
    next_block = lax.ppermute(orbitals, "blk", exchange_pairs(1, blk_size))
    chunk = parts[0] if len(parts) == 1 else jnp.concatenate(parts, 0)

    acc_shape = jax.ShapeDtypeStruct((aux_total, width, columns), jnp.float32)
    table_shape = pltpu.SMEM((2 * slot_total + 6,), jnp.int32)
    small = pltpu.CompilerParams(vmem_limit_bytes=10 << 20)
    ints = integrals

    table = pl.pallas_call(
        functools.partial(sort_kernel, depth, width),
        out_shape=table_shape,
        in_specs=[SMEM, SMEM],
        out_specs=SMEM,
        compiler_params=pltpu.CompilerParams(vmem_limit_bytes=1 << 20),
        cost_estimate=cost(1),
        name="sort",
    )(pair_counts, pair_lists)

    def near(group, coef, *acc):
        return pl.pallas_call(
            functools.partial(near_kernel, group),
            out_shape=acc_shape,
            in_specs=[SMEM, VMEM, VMEM] + [VMEM] * len(acc),
            out_specs=VMEM,
            input_output_aliases={3: 0} if acc else {},
            compiler_params=small,
            cost_estimate=cost(2),
        )(table, ints, coef, *acc)

    acc = near(0, orbitals)
    chunk, acc = lax.optimization_barrier((chunk, acc))
    chunks = [chunk] + [
        lax.ppermute(chunk, ("aux", "occ"), aux_exchange(k, aux_size, occ_size)) for k in range(1, aux_size)
    ]
    acc = near(1, next_block, acc)

    share = width // occ_size
    piece_shape = jax.ShapeDtypeStruct((width, share), jnp.float32)
    halves_shape = jax.ShapeDtypeStruct((width, aux_total * columns), jnp.bfloat16)
    far_scratch = [pltpu.VMEM((aux_size * depth, columns), jnp.bfloat16)]
    far_params = pltpu.CompilerParams(
        vmem_limit_bytes=(10 << 20) + 2 * columns * depth * aux_size
    )
    whole_pairs = (2 * depth) % width == 0
    acc = pl.pallas_call(
        functools.partial(far_kernel, (0, 1)),
        out_shape=acc_shape,
        in_specs=[SMEM] + [VMEM] * 4,
        out_specs=VMEM,
        scratch_shapes=far_scratch,
        input_output_aliases={4: 0},
        compiler_params=far_params,
        cost_estimate=cost(3),
        name="far",
    )(table, ints, *chunks[:2], acc)
    needed = tuple(range(2 if whole_pairs else 0, aux_size))
    _, halves, *pieces = pl.pallas_call(
        functools.partial(last_kernel, needed, occ_size),
        out_shape=[acc_shape, halves_shape] + [piece_shape] * (occ_size - 1),
        in_specs=[SMEM, VMEM] + [VMEM] * (aux_size + 1),
        out_specs=[VMEM] * (occ_size + 1),
        scratch_shapes=far_scratch,
        input_output_aliases={aux_size + 2: 0},
        compiler_params=far_params,
        cost_estimate=cost(3),
        name="last",
    )(table, ints, *chunks, acc)
    kept = pl.pallas_call(
        functools.partial(share_kernel, 0),
        out_shape=piece_shape,
        in_specs=[VMEM],
        out_specs=VMEM,
        compiler_params=small,
        cost_estimate=cost(1),
        name="kept",
    )(halves)

    terms = [kept] + [
        lax.ppermute(pieces[k - 1], "occ", exchange_pairs(k, occ_size)) for k in range(1, occ_size)
    ]
    rows = width // aux_size
    mine = pl.pallas_call(
        split_kernel,
        out_shape=[jax.ShapeDtypeStruct((rows, share), jnp.float32)]
        + [jax.ShapeDtypeStruct((rows + EXPONENT_ROWS, share), jnp.float32)] * (aux_size - 1),
        in_specs=[VMEM] * occ_size,
        out_specs=[VMEM] * aux_size,
        compiler_params=pltpu.CompilerParams(vmem_limit_bytes=8 << 20),
        name="split",
    )(*terms)
    total = mine[0]
    for k in range(1, aux_size):
        sent = mine[k].astype(jnp.float16)
        total = total + unscaled(lax.ppermute(sent, ("aux", "occ"), aux_exchange(k, aux_size, occ_size)), rows)
    total = total / (columns * occ_size)
    shares = [total] + [
        lax.ppermute(total, "occ", exchange_pairs(k, occ_size)) for k in range(1, occ_size)
    ]
    ordered = []
    for o in range(occ_size):
        value = shares[0]
        for k in range(1, occ_size):
            value = jnp.where((my_occ ^ k) == o, shares[k], value)
        ordered.append(value)
    return jnp.concatenate(ordered, 1)[None]


def solution(mesh):
    placed = (P("aux", "blk", None, None, None), P("blk", "occ"), P("blk", None), P("blk"))
    return jax.shard_map(
        per_device, mesh=mesh, in_specs=placed, out_specs=P("blk", "aux", None), check_vma=False
    )
```

```python
import functools
import math

import jax
import jax.numpy as jnp
from jax import lax
from jax.experimental import pallas as pl
from jax.experimental.pallas import tpu as pltpu
from jax.sharding import PartitionSpec as P


ANY = pl.BlockSpec(memory_space=pl.ANY)
VMEM = pl.BlockSpec(memory_space=pltpu.VMEM)
SMEM = pl.BlockSpec(memory_space=pltpu.SMEM)
HBM = pl.BlockSpec(memory_space=pltpu.HBM)


SCALED_TOP = 14
EXPONENT_ROWS = 16


def exchange_pairs(distance, size):
    return [(i, i ^ distance) for i in range(size)]


def mirrored(value, size, core):
    bits = size.bit_length() - 1
    other = sum(((value >> i) & 1) << (bits - 1 - i) for i in range(bits))
    if isinstance(core, int):
        return other if core % 2 else value
    return jnp.where(core % 2 == 1, other, value)


def my_seat():
    return mirrored(lax.axis_index("aux"), lax.axis_size("aux"), lax.axis_index("occ"))


def aux_exchange(distance, aux_size, occ_size):
    return [
        (a * occ_size + c, (a ^ mirrored(distance, aux_size, c)) * occ_size + c)
        for a in range(aux_size)
        for c in range(occ_size)
    ]


def in_hbm(x):
    return pltpu.with_memory_space_constraint(x, pltpu.HBM)


def slot_product(block, coef):
    aux_total, width, _ = block.shape
    product = jnp.dot(
        block.reshape(aux_total * width, width), coef, preferred_element_type=jnp.float32
    )
    return product.reshape(aux_total, width, coef.shape[1])


def add_slots(table, group, ints_ref, coef_rows, acc_ref, fresh=False):
    begin, end = group_bounds(table, group, ints_ref.shape[2])

    def product(i):
        return slot_product(ints_ref[:, 0, table[i]], coef_rows(i))

    if fresh:
        acc_ref[...] = product(0)
        begin = 1
    pairs = (end - begin) // 2

    @pl.loop(0, pairs)
    def _(pair):
        i = begin + 2 * pair
        acc_ref[...] += product(i) + product(i + 1)

    @pl.when(begin + 2 * pairs < end)
    def _():
        acc_ref[...] += product(end - 1)


def group_bounds(table, group, slot_total):
    ends = 2 * slot_total + 2
    return (table[ends + group - 1] if group else 0), table[ends + group]


def head_kernel(piece, t, coef_hbm, out_ref, sem):
    width = coef_hbm.shape[0]
    depth = (lax.axis_size("blk") - 2) * width // lax.axis_size("aux")
    start = lax.rem(my_seat() * depth + t * piece, width)
    rows = pl.ds(pl.multiple_of(start, piece), piece)
    copy = pltpu.make_async_copy(coef_hbm.at[rows], out_ref, sem)
    copy.start()
    copy.wait()


def sort_kernel(far_depth, width, counts, lists, table):
    slot_total = lists.shape[1]
    me, seat = lax.axis_index("blk"), my_seat()
    live = counts[0]
    piece = math.gcd(far_depth, width)
    groups, sizes = [], [jnp.int32(0)] * 4
    for slot in range(slot_total):
        away = lists[0, slot] ^ me
        last = jnp.int32(0)
        for part in range(width // piece):
            last = jnp.maximum(last, lax.div((away - 2) * width + part * piece, far_depth) ^ seat)
        far_group = jnp.where(last <= 1, 2, 3)
        groups.append(jnp.where(slot < live, jnp.where(away < 2, away, far_group), 4))
        sizes = [n + (groups[-1] == g).astype(jnp.int32) for g, n in enumerate(sizes)]
    cursors, found = [], jnp.int32(0)
    for group, size in enumerate(sizes):
        cursors.append(found)
        found = found + size
        table[2 * slot_total + 2 + group] = found
    for slot in range(slot_total):
        place = jnp.int32(slot_total)
        for group in range(4):
            place = jnp.where(groups[slot] == group, cursors[group], place)
        cursors = [n + (groups[slot] == g).astype(jnp.int32) for g, n in enumerate(cursors)]
        table[place] = slot
        table[slot_total + 1 + place] = lists[0, slot] ^ me


def near_kernel(group, table, ints_ref, coef_ref, *accs):
    add_slots(table, group, ints_ref, lambda i: coef_ref[...], accs[-1], fresh=group == 0)


def add_far(group, needed, table, ints_ref, chunks, coef, acc_ref):
    _, _, slot_total, width, _ = ints_ref.shape
    depth = chunks[0].shape[0]
    me = my_seat()
    for k in needed:
        rows = pl.ds(pl.multiple_of((me ^ k) * depth, depth), depth)
        coef[rows, :] = chunks[k][...]

    def coef_rows(i):
        start = (table[slot_total + 1 + i] - 2) * width
        return coef[pl.ds(pl.multiple_of(start, width), width), :]

    add_slots(table, group, ints_ref, coef_rows, acc_ref)


def far_kernel(needed, table, ints_ref, *rest):
    *chunks, _, acc_ref, coef = rest
    add_far(2, needed, table, ints_ref, chunks, coef, acc_ref)


def last_kernel(needed, occ_size, table, ints_ref, *rest):
    *chunks, _, acc_ref, halves = rest[: -occ_size]
    pieces, coef = rest[-occ_size:-1], rest[-1]
    add_far(3, needed, table, ints_ref, chunks, coef, acc_ref)
    columns = acc_ref.shape[2]
    for p in range(acc_ref.shape[0]):
        halves[:, p * columns : (p + 1) * columns] = acc_ref[p].astype(jnp.bfloat16)
    for k, piece_ref in enumerate(pieces, 1):
        share_kernel(k, halves, piece_ref)


def share_kernel(distance, halves, piece_ref):
    share = piece_ref.shape[1]
    start = (lax.axis_index("occ") ^ distance) * share
    rows = pl.ds(pl.multiple_of(start, share), share)
    piece_ref[...] = lax.dot_general(
        halves[...], halves[rows, :], (((1,), (1,)), ((), ())), preferred_element_type=jnp.float32
    )


def split_kernel(*refs):
    aux_size, occ_size = lax.axis_size("aux"), lax.axis_size("occ")
    terms, outs = refs[:occ_size], refs[occ_size:]
    my_aux = lax.axis_index("aux")
    depth = outs[0].shape[0]
    for k in range(aux_size):
        rows = pl.ds(pl.multiple_of((my_aux ^ k) * depth, depth), depth)
        total = terms[0][rows, :]
        for term in terms[1:]:
            total = total + term[rows, :]
        if k == 0:
            outs[k][...] = total
            continue
        peak = jnp.max(jnp.abs(total), axis=0, keepdims=True)
        exponent = jnp.ceil(jnp.log(jnp.maximum(peak, 2.0**-100)) * (1 / math.log(2.0)))
        outs[k][:depth, :] = total * jnp.exp2(SCALED_TOP - exponent)
        outs[k][depth:, :] = jnp.broadcast_to(exponent, (EXPONENT_ROWS, total.shape[1]))


def unscaled(block, depth):
    block = block.astype(jnp.float32)
    return block[:depth] * jnp.exp2(block[depth : depth + 1] - SCALED_TOP)


def per_device(integrals, orbitals, pair_lists, pair_counts):
    aux_total, _, slot_total, width, _ = integrals.shape
    columns = orbitals.shape[1]
    aux_size, blk_size, occ_size = (lax.axis_size(n) for n in ("aux", "blk", "occ"))
    my_occ = lax.axis_index("occ")
    slot_flops = 2 * aux_total * width * width * columns
    slot_bytes = 2 * aux_total * width * width

    def cost(slots):
        return pl.CostEstimate(
            flops=slots * slot_flops, bytes_accessed=slots * slot_bytes, transcendentals=0
        )

    depth = (blk_size - 2) * width // aux_size
    piece = math.gcd(depth, width)
    parts = []
    for t in range(depth // piece):
        pairs = []
        for a in range(aux_size):
            for c in range(occ_size):
                away = 2 + (mirrored(a, aux_size, c) * depth + t * piece) // width
                pairs += [
                    ((a * blk_size + i) * occ_size + c, (a * blk_size + (i ^ away)) * occ_size + c)
                    for i in range(blk_size)
                ]
        sent = pl.pallas_call(
            functools.partial(head_kernel, piece, t),
            out_shape=jax.ShapeDtypeStruct((piece, columns), orbitals.dtype),
            in_specs=[HBM],
            out_specs=VMEM,
            scratch_shapes=[pltpu.SemaphoreType.DMA],
            compiler_params=pltpu.CompilerParams(vmem_limit_bytes=1 << 20),
            cost_estimate=cost(4 * slot_total),
            name="head",
        )(in_hbm(orbitals))
        parts.append(lax.ppermute(sent, ("aux", "blk", "occ"), pairs))
    next_block = lax.ppermute(orbitals, "blk", exchange_pairs(1, blk_size))
    chunk = parts[0] if len(parts) == 1 else jnp.concatenate(parts, 0)

    acc_shape = jax.ShapeDtypeStruct((aux_total, width, columns), jnp.float32)
    table_shape = pltpu.SMEM((2 * slot_total + 6,), jnp.int32)
    small = pltpu.CompilerParams(vmem_limit_bytes=10 << 20)
    ints = integrals

    table = pl.pallas_call(
        functools.partial(sort_kernel, depth, width),
        out_shape=table_shape,
        in_specs=[SMEM, SMEM],
        out_specs=SMEM,
        compiler_params=pltpu.CompilerParams(vmem_limit_bytes=1 << 20),
        cost_estimate=cost(1),
        name="sort",
    )(pair_counts, pair_lists)

    def near(group, coef, *acc):
        return pl.pallas_call(
            functools.partial(near_kernel, group),
            out_shape=acc_shape,
            in_specs=[SMEM, VMEM, VMEM] + [VMEM] * len(acc),
            out_specs=VMEM,
            input_output_aliases={3: 0} if acc else {},
            compiler_params=small,
            cost_estimate=cost(2),
        )(table, ints, coef, *acc)

    acc = near(0, orbitals)
    chunk, acc = lax.optimization_barrier((chunk, acc))
    chunks = [chunk] + [
        lax.ppermute(chunk, ("aux", "occ"), aux_exchange(k, aux_size, occ_size)) for k in range(1, aux_size)
    ]
    acc = near(1, next_block, acc)

    share = width // occ_size
    piece_shape = jax.ShapeDtypeStruct((width, share), jnp.float32)
    halves_shape = jax.ShapeDtypeStruct((width, aux_total * columns), jnp.bfloat16)
    far_scratch = [pltpu.VMEM((aux_size * depth, columns), jnp.bfloat16)]
    far_params = pltpu.CompilerParams(
        vmem_limit_bytes=(10 << 20) + 2 * columns * depth * aux_size
    )
    whole_pairs = (2 * depth) % width == 0
    acc = pl.pallas_call(
        functools.partial(far_kernel, (0, 1)),
        out_shape=acc_shape,
        in_specs=[SMEM] + [VMEM] * 4,
        out_specs=VMEM,
        scratch_shapes=far_scratch,
        input_output_aliases={4: 0},
        compiler_params=far_params,
        cost_estimate=cost(3),
        name="far",
    )(table, ints, *chunks[:2], acc)
    needed = tuple(range(2 if whole_pairs else 0, aux_size))
    _, halves, *pieces = pl.pallas_call(
        functools.partial(last_kernel, needed, occ_size),
        out_shape=[acc_shape, halves_shape] + [piece_shape] * (occ_size - 1),
        in_specs=[SMEM, VMEM] + [VMEM] * (aux_size + 1),
        out_specs=[VMEM] * (occ_size + 1),
        scratch_shapes=far_scratch,
        input_output_aliases={aux_size + 2: 0},
        compiler_params=far_params,
        cost_estimate=cost(3),
        name="last",
    )(table, ints, *chunks, acc)
    kept = pl.pallas_call(
        functools.partial(share_kernel, 0),
        out_shape=piece_shape,
        in_specs=[VMEM],
        out_specs=VMEM,
        compiler_params=small,
        cost_estimate=cost(1),
        name="kept",
    )(halves)

    terms = [kept] + [
        lax.ppermute(pieces[k - 1], "occ", exchange_pairs(k, occ_size)) for k in range(1, occ_size)
    ]
    rows = width // aux_size
    mine = pl.pallas_call(
        split_kernel,
        out_shape=[jax.ShapeDtypeStruct((rows, share), jnp.float32)]
        + [jax.ShapeDtypeStruct((rows + EXPONENT_ROWS, share), jnp.float32)] * (aux_size - 1),
        in_specs=[VMEM] * occ_size,
        out_specs=[VMEM] * aux_size,
        compiler_params=pltpu.CompilerParams(vmem_limit_bytes=8 << 20),
        name="split",
    )(*terms)
    total = mine[0]
    for k in range(1, aux_size):
        sent = mine[k].astype(jnp.float16)
        total = total + unscaled(lax.ppermute(sent, "aux", exchange_pairs(k, aux_size)), rows)
    total = total / (columns * occ_size)
    shares = [total] + [
        lax.ppermute(total, "occ", exchange_pairs(k, occ_size)) for k in range(1, occ_size)
    ]
    ordered = []
    for o in range(occ_size):
        value = shares[0]
        for k in range(1, occ_size):
            value = jnp.where((my_occ ^ k) == o, shares[k], value)
        ordered.append(value)
    return jnp.concatenate(ordered, 1)[None]


def solution(mesh):
    placed = (P("aux", "blk", None, None, None), P("blk", "occ"), P("blk", None), P("blk"))
    return jax.shard_map(
        per_device, mesh=mesh, in_specs=placed, out_specs=P("blk", "aux", None), check_vma=False
    )
```

```python
import functools
import math

import jax
import jax.numpy as jnp
from jax import lax
from jax.experimental import pallas as pl
from jax.experimental.pallas import tpu as pltpu
from jax.sharding import PartitionSpec as P


ANY = pl.BlockSpec(memory_space=pl.ANY)
VMEM = pl.BlockSpec(memory_space=pltpu.VMEM)
SMEM = pl.BlockSpec(memory_space=pltpu.SMEM)
HBM = pl.BlockSpec(memory_space=pltpu.HBM)


SCALED_TOP = 14
EXPONENT_ROWS = 16


def exchange_pairs(distance, size):
    return [(i, i ^ distance) for i in range(size)]


def mirrored(value, size, core):
    bits = size.bit_length() - 1
    other = sum(((value >> i) & 1) << (bits - 1 - i) for i in range(bits))
    if isinstance(core, int):
        return other if core % 2 else value
    return jnp.where(core % 2 == 1, other, value)


def my_seat():
    return mirrored(lax.axis_index("aux"), lax.axis_size("aux"), lax.axis_index("occ"))


def aux_exchange(distance, aux_size, occ_size):
    return [
        (a * occ_size + c, (a ^ mirrored(distance, aux_size, c)) * occ_size + c)
        for a in range(aux_size)
        for c in range(occ_size)
    ]


def in_hbm(x):
    return pltpu.with_memory_space_constraint(x, pltpu.HBM)


def slot_product(block, coef):
    aux_total, width, _ = block.shape
    product = jnp.dot(
        block.reshape(aux_total * width, width), coef, preferred_element_type=jnp.float32
    )
    return product.reshape(aux_total, width, coef.shape[1])


GROUPS = 5
OWN_FIRST = 3


def add_slots(table, group, ints_ref, coef_rows, acc_ref, fresh=False):
    begin, end = group_bounds(table, group, ints_ref.shape[2])

    def product(i):
        return slot_product(ints_ref[:, 0, table[i]], coef_rows(i))

    if fresh:
        acc_ref[...] = product(0)
        begin = 1
    pairs = (end - begin) // 2

    @pl.loop(0, pairs)
    def _(pair):
        i = begin + 2 * pair
        acc_ref[...] += product(i) + product(i + 1)

    @pl.when(begin + 2 * pairs < end)
    def _():
        acc_ref[...] += product(end - 1)


def group_bounds(table, group, slot_total):
    ends = 2 * slot_total + 2
    return (table[ends + group - 1] if group else 0), table[ends + group]


def head_kernel(piece, t, coef_hbm, out_ref, sem):
    width = coef_hbm.shape[0]
    depth = (lax.axis_size("blk") - 2) * width // lax.axis_size("aux")
    start = lax.rem(my_seat() * depth + t * piece, width)
    rows = pl.ds(pl.multiple_of(start, piece), piece)
    copy = pltpu.make_async_copy(coef_hbm.at[rows], out_ref, sem)
    copy.start()
    copy.wait()


def sort_kernel(far_depth, width, counts, lists, table):
    slot_total = lists.shape[1]
    me, seat = lax.axis_index("blk"), my_seat()
    live = counts[0]
    piece = math.gcd(far_depth, width)
    groups, sizes = [], [jnp.int32(0)] * GROUPS
    for slot in range(slot_total):
        away = lists[0, slot] ^ me
        last = jnp.int32(0)
        for part in range(width // piece):
            last = jnp.maximum(last, lax.div((away - 2) * width + part * piece, far_depth) ^ seat)
        own_group = jnp.where(sizes[0] < OWN_FIRST, 0, 1)
        group = jnp.where(away < 2, jnp.where(away == 0, own_group, 2), jnp.where(last <= 1, 3, 4))
        groups.append(jnp.where(slot < live, group, GROUPS))
        sizes = [n + (groups[-1] == g).astype(jnp.int32) for g, n in enumerate(sizes)]
    cursors, found = [], jnp.int32(0)
    for group, size in enumerate(sizes):
        cursors.append(found)
        found = found + size
        table[2 * slot_total + 2 + group] = found
    for slot in range(slot_total):
        place = jnp.int32(slot_total)
        for group in range(GROUPS):
            place = jnp.where(groups[slot] == group, cursors[group], place)
        cursors = [n + (groups[slot] == g).astype(jnp.int32) for g, n in enumerate(cursors)]
        table[place] = slot
        table[slot_total + 1 + place] = lists[0, slot] ^ me


def near_kernel(groups, table, ints_ref, *rest):
    coefs, acc_ref = rest[: len(groups)], rest[-1]
    for group, coef_ref in zip(groups, coefs):
        add_slots(table, group, ints_ref, lambda i: coef_ref[...], acc_ref, fresh=group == 0)


def add_far(group, needed, table, ints_ref, chunks, coef, acc_ref):
    _, _, slot_total, width, _ = ints_ref.shape
    depth = chunks[0].shape[0]
    me = my_seat()
    for k in needed:
        rows = pl.ds(pl.multiple_of((me ^ k) * depth, depth), depth)
        coef[rows, :] = chunks[k][...]

    def coef_rows(i):
        start = (table[slot_total + 1 + i] - 2) * width
        return coef[pl.ds(pl.multiple_of(start, width), width), :]

    add_slots(table, group, ints_ref, coef_rows, acc_ref)


def far_kernel(needed, table, ints_ref, *rest):
    *chunks, _, acc_ref, coef = rest
    add_far(3, needed, table, ints_ref, chunks, coef, acc_ref)


def last_kernel(needed, occ_size, table, ints_ref, *rest):
    *chunks, _, acc_ref, halves = rest[: -occ_size]
    pieces, coef = rest[-occ_size:-1], rest[-1]
    add_far(4, needed, table, ints_ref, chunks, coef, acc_ref)
    columns = acc_ref.shape[2]
    for p in range(acc_ref.shape[0]):
        halves[:, p * columns : (p + 1) * columns] = acc_ref[p].astype(jnp.bfloat16)
    for k, piece_ref in enumerate(pieces, 1):
        share_kernel(k, halves, piece_ref)


def share_kernel(distance, halves, piece_ref):
    share = piece_ref.shape[1]
    start = (lax.axis_index("occ") ^ distance) * share
    rows = pl.ds(pl.multiple_of(start, share), share)
    piece_ref[...] = lax.dot_general(
        halves[...], halves[rows, :], (((1,), (1,)), ((), ())), preferred_element_type=jnp.float32
    )


def split_kernel(*refs):
    aux_size, occ_size = lax.axis_size("aux"), lax.axis_size("occ")
    terms, outs = refs[:occ_size], refs[occ_size:]
    my_aux = lax.axis_index("aux")
    depth = outs[0].shape[0]
    for k in range(aux_size):
        rows = pl.ds(pl.multiple_of((my_aux ^ k) * depth, depth), depth)
        total = terms[0][rows, :]
        for term in terms[1:]:
            total = total + term[rows, :]
        if k == 0:
            outs[k][...] = total
            continue
        peak = jnp.max(jnp.abs(total), axis=0, keepdims=True)
        exponent = jnp.ceil(jnp.log(jnp.maximum(peak, 2.0**-100)) * (1 / math.log(2.0)))
        outs[k][:depth, :] = total * jnp.exp2(SCALED_TOP - exponent)
        outs[k][depth:, :] = jnp.broadcast_to(exponent, (EXPONENT_ROWS, total.shape[1]))


def unscaled(block, depth):
    block = block.astype(jnp.float32)
    return block[:depth] * jnp.exp2(block[depth : depth + 1] - SCALED_TOP)


def per_device(integrals, orbitals, pair_lists, pair_counts):
    aux_total, _, slot_total, width, _ = integrals.shape
    columns = orbitals.shape[1]
    aux_size, blk_size, occ_size = (lax.axis_size(n) for n in ("aux", "blk", "occ"))
    my_occ = lax.axis_index("occ")
    slot_flops = 2 * aux_total * width * width * columns
    slot_bytes = 2 * aux_total * width * width

    def cost(slots):
        return pl.CostEstimate(
            flops=slots * slot_flops, bytes_accessed=slots * slot_bytes, transcendentals=0
        )

    depth = (blk_size - 2) * width // aux_size
    piece = math.gcd(depth, width)
    parts = []
    for t in range(depth // piece):
        pairs = []
        for a in range(aux_size):
            for c in range(occ_size):
                away = 2 + (mirrored(a, aux_size, c) * depth + t * piece) // width
                pairs += [
                    ((a * blk_size + i) * occ_size + c, (a * blk_size + (i ^ away)) * occ_size + c)
                    for i in range(blk_size)
                ]
        sent = pl.pallas_call(
            functools.partial(head_kernel, piece, t),
            out_shape=jax.ShapeDtypeStruct((piece, columns), orbitals.dtype),
            in_specs=[HBM],
            out_specs=VMEM,
            scratch_shapes=[pltpu.SemaphoreType.DMA],
            compiler_params=pltpu.CompilerParams(vmem_limit_bytes=1 << 20),
            cost_estimate=cost(4 * slot_total),
            name="head",
        )(in_hbm(orbitals))
        parts.append(lax.ppermute(sent, ("aux", "blk", "occ"), pairs))
    next_block = lax.ppermute(orbitals, "blk", exchange_pairs(1, blk_size))
    chunk = parts[0] if len(parts) == 1 else jnp.concatenate(parts, 0)

    acc_shape = jax.ShapeDtypeStruct((aux_total, width, columns), jnp.float32)
    table_shape = pltpu.SMEM((2 * slot_total + 2 + GROUPS,), jnp.int32)
    small = pltpu.CompilerParams(vmem_limit_bytes=10 << 20)
    ints = integrals

    table = pl.pallas_call(
        functools.partial(sort_kernel, depth, width),
        out_shape=table_shape,
        in_specs=[SMEM, SMEM],
        out_specs=SMEM,
        compiler_params=pltpu.CompilerParams(vmem_limit_bytes=1 << 20),
        cost_estimate=cost(1),
        name="sort",
    )(pair_counts, pair_lists)

    def near(groups, coefs, *acc):
        return pl.pallas_call(
            functools.partial(near_kernel, groups),
            out_shape=acc_shape,
            in_specs=[SMEM, VMEM] + [VMEM] * (len(coefs) + len(acc)),
            out_specs=VMEM,
            input_output_aliases={2 + len(coefs): 0} if acc else {},
            compiler_params=small,
            cost_estimate=cost(2),
        )(table, ints, *coefs, *acc)

    acc = near((0,), (orbitals,))
    chunk, acc = lax.optimization_barrier((chunk, acc))
    chunks = [chunk] + [
        lax.ppermute(chunk, ("aux", "occ"), aux_exchange(k, aux_size, occ_size)) for k in range(1, aux_size)
    ]
    acc = near((1, 2), (orbitals, next_block), acc)

    share = width // occ_size
    piece_shape = jax.ShapeDtypeStruct((width, share), jnp.float32)
    halves_shape = jax.ShapeDtypeStruct((width, aux_total * columns), jnp.bfloat16)
    far_scratch = [pltpu.VMEM((aux_size * depth, columns), jnp.bfloat16)]
    far_params = pltpu.CompilerParams(
        vmem_limit_bytes=(10 << 20) + 2 * columns * depth * aux_size
    )
    whole_pairs = (2 * depth) % width == 0
    acc = pl.pallas_call(
        functools.partial(far_kernel, (0, 1)),
        out_shape=acc_shape,
        in_specs=[SMEM] + [VMEM] * 4,
        out_specs=VMEM,
        scratch_shapes=far_scratch,
        input_output_aliases={4: 0},
        compiler_params=far_params,
        cost_estimate=cost(3),
        name="far",
    )(table, ints, *chunks[:2], acc)
    needed = tuple(range(2 if whole_pairs else 0, aux_size))
    _, halves, *pieces = pl.pallas_call(
        functools.partial(last_kernel, needed, occ_size),
        out_shape=[acc_shape, halves_shape] + [piece_shape] * (occ_size - 1),
        in_specs=[SMEM, VMEM] + [VMEM] * (aux_size + 1),
        out_specs=[VMEM] * (occ_size + 1),
        scratch_shapes=far_scratch,
        input_output_aliases={aux_size + 2: 0},
        compiler_params=far_params,
        cost_estimate=cost(3),
        name="last",
    )(table, ints, *chunks, acc)
    kept = pl.pallas_call(
        functools.partial(share_kernel, 0),
        out_shape=piece_shape,
        in_specs=[VMEM],
        out_specs=VMEM,
        compiler_params=small,
        cost_estimate=cost(1),
        name="kept",
    )(halves)

    terms = [kept] + [
        lax.ppermute(pieces[k - 1], "occ", exchange_pairs(k, occ_size)) for k in range(1, occ_size)
    ]
    rows = width // aux_size
    mine = pl.pallas_call(
        split_kernel,
        out_shape=[jax.ShapeDtypeStruct((rows, share), jnp.float32)]
        + [jax.ShapeDtypeStruct((rows + EXPONENT_ROWS, share), jnp.float32)] * (aux_size - 1),
        in_specs=[VMEM] * occ_size,
        out_specs=[VMEM] * aux_size,
        compiler_params=pltpu.CompilerParams(vmem_limit_bytes=8 << 20),
        name="split",
    )(*terms)
    total = mine[0]
    for k in range(1, aux_size):
        sent = mine[k].astype(jnp.float16)
        total = total + unscaled(lax.ppermute(sent, "aux", exchange_pairs(k, aux_size)), rows)
    total = total / (columns * occ_size)
    shares = [total] + [
        lax.ppermute(total, "occ", exchange_pairs(k, occ_size)) for k in range(1, occ_size)
    ]
    ordered = []
    for o in range(occ_size):
        value = shares[0]
        for k in range(1, occ_size):
            value = jnp.where((my_occ ^ k) == o, shares[k], value)
        ordered.append(value)
    return jnp.concatenate(ordered, 1)[None]


def solution(mesh):
    placed = (P("aux", "blk", None, None, None), P("blk", "occ"), P("blk", None), P("blk"))
    return jax.shard_map(
        per_device, mesh=mesh, in_specs=placed, out_specs=P("blk", "aux", None), check_vma=False
    )
```

```python
import functools
import math

import jax
import jax.numpy as jnp
from jax import lax
from jax.experimental import pallas as pl
from jax.experimental.pallas import tpu as pltpu
from jax.sharding import PartitionSpec as P


ANY = pl.BlockSpec(memory_space=pl.ANY)
VMEM = pl.BlockSpec(memory_space=pltpu.VMEM)
SMEM = pl.BlockSpec(memory_space=pltpu.SMEM)
HBM = pl.BlockSpec(memory_space=pltpu.HBM)


SCALED_TOP = 14
EXPONENT_ROWS = 16


def exchange_pairs(distance, size):
    return [(i, i ^ distance) for i in range(size)]


def mirrored(value, size, core):
    bits = size.bit_length() - 1
    other = sum(((value >> i) & 1) << (bits - 1 - i) for i in range(bits))
    if isinstance(core, int):
        return other if core % 2 else value
    return jnp.where(core % 2 == 1, other, value)


def my_seat():
    return mirrored(lax.axis_index("aux"), lax.axis_size("aux"), lax.axis_index("occ"))


def aux_exchange(distance, aux_size, occ_size):
    return [
        (a * occ_size + c, (a ^ mirrored(distance, aux_size, c)) * occ_size + c)
        for a in range(aux_size)
        for c in range(occ_size)
    ]


def in_hbm(x):
    return pltpu.with_memory_space_constraint(x, pltpu.HBM)


def slot_product(block, coef):
    aux_total, width, _ = block.shape
    product = jnp.dot(
        block.reshape(aux_total * width, width), coef, preferred_element_type=jnp.float32
    )
    return product.reshape(aux_total, width, coef.shape[1])


def add_slots(table, group, ints_ref, coef_rows, acc_ref, fresh=False):
    begin, end = group_bounds(table, group, ints_ref.shape[2])

    def product(i):
        return slot_product(ints_ref[:, 0, table[i]], coef_rows(i))

    if fresh:
        acc_ref[...] = product(0)
        begin = 1
    pairs = (end - begin) // 2

    @pl.loop(0, pairs)
    def _(pair):
        i = begin + 2 * pair
        acc_ref[...] += product(i) + product(i + 1)

    @pl.when(begin + 2 * pairs < end)
    def _():
        acc_ref[...] += product(end - 1)


def group_bounds(table, group, slot_total):
    ends = 2 * slot_total + 2
    return (table[ends + group - 1] if group else 0), table[ends + group]


def head_kernel(piece, t, coef_hbm, out_ref, sem):
    width = coef_hbm.shape[0]
    depth = (lax.axis_size("blk") - 2) * width // lax.axis_size("aux")
    start = lax.rem(my_seat() * depth + t * piece, width)
    rows = pl.ds(pl.multiple_of(start, piece), piece)
    copy = pltpu.make_async_copy(coef_hbm.at[rows], out_ref, sem)
    copy.start()
    copy.wait()


def sort_kernel(far_depth, width, counts, lists, table):
    slot_total = lists.shape[1]
    me, seat = lax.axis_index("blk"), my_seat()
    live = counts[0]
    piece = math.gcd(far_depth, width)
    groups, sizes = [], [jnp.int32(0)] * 4
    for slot in range(slot_total):
        away = lists[0, slot] ^ me
        last = jnp.int32(0)
        for part in range(width // piece):
            last = jnp.maximum(last, lax.div((away - 2) * width + part * piece, far_depth) ^ seat)
        far_group = jnp.where(last <= 1, 2, 3)
        groups.append(jnp.where(slot < live, jnp.where(away < 2, away, far_group), 4))
        sizes = [n + (groups[-1] == g).astype(jnp.int32) for g, n in enumerate(sizes)]
    cursors, found = [], jnp.int32(0)
    for group, size in enumerate(sizes):
        cursors.append(found)
        found = found + size
        table[2 * slot_total + 2 + group] = found
    for slot in range(slot_total):
        place = jnp.int32(slot_total)
        for group in range(4):
            place = jnp.where(groups[slot] == group, cursors[group], place)
        cursors = [n + (groups[slot] == g).astype(jnp.int32) for g, n in enumerate(cursors)]
        table[place] = slot
        table[slot_total + 1 + place] = lists[0, slot] ^ me


def near_kernel(group, table, ints_ref, coef_ref, *accs):
    add_slots(table, group, ints_ref, lambda i: coef_ref[...], accs[-1], fresh=group == 0)


def add_far(group, needed, table, ints_ref, chunks, coef, acc_ref):
    _, _, slot_total, width, _ = ints_ref.shape
    depth = chunks[0].shape[0]
    me = my_seat()
    for k in needed:
        rows = pl.ds(pl.multiple_of((me ^ k) * depth, depth), depth)
        coef[rows, :] = chunks[k][...]

    def coef_rows(i):
        start = (table[slot_total + 1 + i] - 2) * width
        return coef[pl.ds(pl.multiple_of(start, width), width), :]

    add_slots(table, group, ints_ref, coef_rows, acc_ref)


def far_kernel(needed, table, ints_ref, *rest):
    *chunks, _, acc_ref, coef = rest
    add_far(2, needed, table, ints_ref, chunks, coef, acc_ref)


def last_kernel(needed, occ_size, table, ints_ref, *rest):
    *chunks, _, acc_ref, halves = rest[: -occ_size]
    pieces, coef = rest[-occ_size:-1], rest[-1]
    add_far(3, needed, table, ints_ref, chunks, coef, acc_ref)
    columns = acc_ref.shape[2]
    for p in range(acc_ref.shape[0]):
        halves[:, p * columns : (p + 1) * columns] = acc_ref[p].astype(jnp.bfloat16)
    for k, piece_ref in enumerate(pieces, 1):
        share_kernel(k, halves, piece_ref)


def share_kernel(distance, halves, piece_ref):
    share = piece_ref.shape[1]
    start = (lax.axis_index("occ") ^ distance) * share
    rows = pl.ds(pl.multiple_of(start, share), share)
    piece_ref[...] = lax.dot_general(
        halves[...], halves[rows, :], (((1,), (1,)), ((), ())), preferred_element_type=jnp.float32
    )


def split_kernel(*refs):
    aux_size, occ_size = lax.axis_size("aux"), lax.axis_size("occ")
    terms, outs = refs[:occ_size], refs[occ_size:]
    my_aux = lax.axis_index("aux")
    depth = outs[0].shape[0]
    for k in range(aux_size):
        rows = pl.ds(pl.multiple_of((my_aux ^ k) * depth, depth), depth)
        total = terms[0][rows, :]
        for term in terms[1:]:
            total = total + term[rows, :]
        if k == 0:
            outs[k][...] = total
            continue
        peak = jnp.max(jnp.abs(total), axis=0, keepdims=True)
        exponent = jnp.ceil(jnp.log(jnp.maximum(peak, 2.0**-100)) * (1 / math.log(2.0)))
        outs[k][:depth, :] = total * jnp.exp2(SCALED_TOP - exponent)
        outs[k][depth:, :] = jnp.broadcast_to(exponent, (EXPONENT_ROWS, total.shape[1]))


def unscaled(block, depth):
    block = block.astype(jnp.float32)
    return block[:depth] * jnp.exp2(block[depth : depth + 1] - SCALED_TOP)


def join_kernel(*refs):
    *shares, out_ref, sems = refs
    width = shares[0].shape[1]
    copies = []
    for k, share in enumerate(shares):
        start = (lax.axis_index("occ") ^ k) * width
        columns = pl.ds(pl.multiple_of(start, width), width)
        copies.append(pltpu.make_async_copy(share, out_ref.at[0, :, columns], sems.at[k]))
    for copy in copies:
        copy.start()
    for copy in copies:
        copy.wait()


def per_device(integrals, orbitals, pair_lists, pair_counts):
    aux_total, _, slot_total, width, _ = integrals.shape
    columns = orbitals.shape[1]
    aux_size, blk_size, occ_size = (lax.axis_size(n) for n in ("aux", "blk", "occ"))
    slot_flops = 2 * aux_total * width * width * columns
    slot_bytes = 2 * aux_total * width * width

    def cost(slots):
        return pl.CostEstimate(
            flops=slots * slot_flops, bytes_accessed=slots * slot_bytes, transcendentals=0
        )

    depth = (blk_size - 2) * width // aux_size
    piece = math.gcd(depth, width)
    parts = []
    for t in range(depth // piece):
        pairs = []
        for a in range(aux_size):
            for c in range(occ_size):
                away = 2 + (mirrored(a, aux_size, c) * depth + t * piece) // width
                pairs += [
                    ((a * blk_size + i) * occ_size + c, (a * blk_size + (i ^ away)) * occ_size + c)
                    for i in range(blk_size)
                ]
        sent = pl.pallas_call(
            functools.partial(head_kernel, piece, t),
            out_shape=jax.ShapeDtypeStruct((piece, columns), orbitals.dtype),
            in_specs=[HBM],
            out_specs=VMEM,
            scratch_shapes=[pltpu.SemaphoreType.DMA],
            compiler_params=pltpu.CompilerParams(vmem_limit_bytes=1 << 20),
            cost_estimate=cost(4 * slot_total),
            name="head",
        )(in_hbm(orbitals))
        parts.append(lax.ppermute(sent, ("aux", "blk", "occ"), pairs))
    next_block = lax.ppermute(orbitals, "blk", exchange_pairs(1, blk_size))
    chunk = parts[0] if len(parts) == 1 else jnp.concatenate(parts, 0)

    acc_shape = jax.ShapeDtypeStruct((aux_total, width, columns), jnp.float32)
    table_shape = pltpu.SMEM((2 * slot_total + 6,), jnp.int32)
    small = pltpu.CompilerParams(vmem_limit_bytes=10 << 20)
    ints = integrals

    table = pl.pallas_call(
        functools.partial(sort_kernel, depth, width),
        out_shape=table_shape,
        in_specs=[SMEM, SMEM],
        out_specs=SMEM,
        compiler_params=pltpu.CompilerParams(vmem_limit_bytes=1 << 20),
        cost_estimate=cost(1),
        name="sort",
    )(pair_counts, pair_lists)

    def near(group, coef, *acc):
        return pl.pallas_call(
            functools.partial(near_kernel, group),
            out_shape=acc_shape,
            in_specs=[SMEM, VMEM, VMEM] + [VMEM] * len(acc),
            out_specs=VMEM,
            input_output_aliases={3: 0} if acc else {},
            compiler_params=small,
            cost_estimate=cost(2),
        )(table, ints, coef, *acc)

    acc = near(0, orbitals)
    chunk, acc = lax.optimization_barrier((chunk, acc))
    chunks = [chunk] + [
        lax.ppermute(chunk, ("aux", "occ"), aux_exchange(k, aux_size, occ_size)) for k in range(1, aux_size)
    ]
    acc = near(1, next_block, acc)

    share = width // occ_size
    piece_shape = jax.ShapeDtypeStruct((width, share), jnp.float32)
    halves_shape = jax.ShapeDtypeStruct((width, aux_total * columns), jnp.bfloat16)
    far_scratch = [pltpu.VMEM((aux_size * depth, columns), jnp.bfloat16)]
    far_params = pltpu.CompilerParams(
        vmem_limit_bytes=(10 << 20) + 2 * columns * depth * aux_size
    )
    whole_pairs = (2 * depth) % width == 0
    acc = pl.pallas_call(
        functools.partial(far_kernel, (0, 1)),
        out_shape=acc_shape,
        in_specs=[SMEM] + [VMEM] * 4,
        out_specs=VMEM,
        scratch_shapes=far_scratch,
        input_output_aliases={4: 0},
        compiler_params=far_params,
        cost_estimate=cost(3),
        name="far",
    )(table, ints, *chunks[:2], acc)
    needed = tuple(range(2 if whole_pairs else 0, aux_size))
    _, halves, *pieces = pl.pallas_call(
        functools.partial(last_kernel, needed, occ_size),
        out_shape=[acc_shape, halves_shape] + [piece_shape] * (occ_size - 1),
        in_specs=[SMEM, VMEM] + [VMEM] * (aux_size + 1),
        out_specs=[VMEM] * (occ_size + 1),
        scratch_shapes=far_scratch,
        input_output_aliases={aux_size + 2: 0},
        compiler_params=far_params,
        cost_estimate=cost(3),
        name="last",
    )(table, ints, *chunks, acc)
    kept = pl.pallas_call(
        functools.partial(share_kernel, 0),
        out_shape=piece_shape,
        in_specs=[VMEM],
        out_specs=VMEM,
        compiler_params=small,
        cost_estimate=cost(1),
        name="kept",
    )(halves)

    terms = [kept] + [
        lax.ppermute(pieces[k - 1], "occ", exchange_pairs(k, occ_size)) for k in range(1, occ_size)
    ]
    rows = width // aux_size
    mine = pl.pallas_call(
        split_kernel,
        out_shape=[jax.ShapeDtypeStruct((rows, share), jnp.float32)]
        + [jax.ShapeDtypeStruct((rows + EXPONENT_ROWS, share), jnp.float32)] * (aux_size - 1),
        in_specs=[VMEM] * occ_size,
        out_specs=[VMEM] * aux_size,
        compiler_params=pltpu.CompilerParams(vmem_limit_bytes=8 << 20),
        name="split",
    )(*terms)
    total = mine[0]
    for k in range(1, aux_size):
        sent = mine[k].astype(jnp.float16)
        total = total + unscaled(lax.ppermute(sent, "aux", exchange_pairs(k, aux_size)), rows)
    total = total / (columns * occ_size)
    shares = [total] + [
        lax.ppermute(total, "occ", exchange_pairs(k, occ_size)) for k in range(1, occ_size)
    ]
    return pl.pallas_call(
        join_kernel,
        out_shape=jax.ShapeDtypeStruct((1, rows, width), jnp.float32),
        in_specs=[VMEM] * occ_size,
        out_specs=HBM,
        scratch_shapes=[pltpu.SemaphoreType.DMA((occ_size,))],
        compiler_params=pltpu.CompilerParams(vmem_limit_bytes=1 << 20),
        name="join",
    )(*shares)


def solution(mesh):
    placed = (P("aux", "blk", None, None, None), P("blk", "occ"), P("blk", None), P("blk"))
    return jax.shard_map(
        per_device, mesh=mesh, in_specs=placed, out_specs=P("blk", "aux", None), check_vma=False
    )
```
